128 devices in a mesh: tensor: 8 (over y, core), adapter: 16 (over x, z).
Axes of the slice: x: 4, y: 4, z: 4, core: 2. Of those that a mesh axis runs over, the one named last changes fastest.
Arguments:
- tokens_in: bfloat16 [512, 8192], P(('tensor', 'adapter')), may hold values from -6 to 6
- w_gate: bfloat16 [8192, 28672], P(None, ('tensor', 'adapter')), may hold values from -0.0625 to 0.0625
- w_up: bfloat16 [8192, 28672], P(None, ('tensor', 'adapter')), may hold values from -0.0625 to 0.0625
- w_down: bfloat16 [28672, 8192], P('tensor', 'adapter'), may hold values from -0.03125 to 0.03125
- a_gate: bfloat16 [8192, 2048], P(None, 'adapter'), may hold values from -0.0625 to 0.0625
- a_up: bfloat16 [8192, 2048], P(None, 'adapter'), may hold values from -0.0625 to 0.0625
- b_gate: bfloat16 [2048, 28672], P(None, ('tensor', 'adapter')), may hold values from -1.5 to 1.5
- b_up: bfloat16 [2048, 28672], P(None, ('tensor', 'adapter')), may hold values from -1.5 to 1.5
- a_down: bfloat16 [28672, 2048], P(('tensor', 'adapter')), may hold values from -0.03125 to 0.03125
- b_down: bfloat16 [2048, 8192], P('adapter'), may hold values from -1.5 to 1.5
- lengths: int32 [8], replicated, may hold values from 1 to 128, 512 in all
- request_adapter: int32 [8], replicated, may hold values from 0 to 127
- placement: int32 [128], replicated, may hold values from 0 to 127, each once
Outputs:
- mixed: bfloat16 [512, 8192], P(('tensor', 'adapter'))
The draws below stay inside these ranges and needn't reach their ends.
Inputs may be any that keep to these rules, and one draw needn't show every extreme that they name: The 8 lengths sum to 512; the longest is exactly 512 // 4. `placement`: each storage slot holds exactly one adapter.
All inputs are finite; a program needn't handle non-finite values.
Results may differ from the reference program's by a relative error of at most 0.0085.
Values may be sent and summed in bfloat16 or wider, within the bound.
No kernel may reach another device: no remote copies, remote signals or barrier semaphores. Data moves between devices by JAX's collectives and lax.ppermute only.
A program may use at most 128 MiB of HBM per device.

```python
import math
import jax
import jax.numpy as jnp
import numpy as np

D = 8192
FF = 28672
R = 16
REQS = 8
TOKENS = 512
ADAPTERS = 128


def with_ends(values, stream_key, least, top_value):
    longest = values.shape.index(max(values.shape))
    spots = []
    for shift in (0, 1):
        where = [jax.random.randint(jax.random.fold_in(stream_key, axis), (), 0, length) for axis, length in enumerate(values.shape)]
        where[longest] = (where[longest] + shift) % values.shape[longest]
        spots.append(tuple(where))
    return values.at[spots[0]].set(least).at[spots[1]].set(top_value)


def shard_levels(stream_key, dims, cuts, least, top_value):
    loudness, own = 1.0, jax.random.fold_in(stream_key, 6)
    for axis_at, parts in cuts:
        draws = jnp.exp(jax.random.uniform(jax.random.fold_in(own, axis_at), (parts,), jnp.float32, least / len(cuts), top_value / len(cuts)))
        loudness = loudness * jnp.repeat(draws, dims[axis_at] // parts).reshape([-1 if axis == axis_at else 1 for axis in range(len(dims))])
    return loudness


def length_profile(count, total, most, lean):
    loads = [(1 << 20) // math.isqrt(rank ** lean) + 1 for rank in range(2, count + 1)]
    rest, given = total - most - (count - 1), [1] * (count - 1)
    while rest > 0:
        candidates = [i for i in range(count - 1) if given[i] < most]
        pool, budget = sum([loads[i] for i in candidates]), rest
        for i in candidates:
            extra = min(most - given[i], max(1, budget * loads[i] // pool), rest)
            given[i] = given[i] + extra
            rest = rest - extra
    return np.array([most] + given)


def uneven(key, count, total, bound, lean):
    if count == 2:
        one = jax.random.randint(key, (), max(1, total - bound), min(bound, total - 1) + 1)
        return jnp.stack([one, total - one])
    sizes = jnp.asarray(length_profile(count, total, bound, lean), jnp.int32)
    twos = (count - 1) // 2
    source_of, receiver = sizes[1:1 + 2 * twos:2], sizes[2:2 + 2 * twos:2]
    room = jnp.minimum(source_of - 1, bound - receiver)
    passed = jax.random.randint(jax.random.fold_in(key, 1), (twos,), 0, 1 << 20) % (room + 1)
    sizes = sizes.at[1:1 + 2 * twos:2].set(source_of - passed).at[2:2 + 2 * twos:2].set(receiver + passed)
    return sizes[jax.random.permutation(jax.random.fold_in(key, 2), count)]


def scatter_about(key, extent, deviation, bound, cuts=(), kind=jnp.bfloat16):
    loudness = shard_levels(key, extent, cuts, -0.22, 0.18) if cuts else 1.0
    result = jax.random.normal(key, extent, jnp.float32) * deviation * loudness
    return jnp.minimum(jnp.maximum(result, -bound), bound).astype(kind)


def setup_inputs(seed: int = 0) -> dict:
    arg_keys = jax.random.split(jax.random.key(seed), 14)
    return {
        "tokens_in": scatter_about(arg_keys[0], (TOKENS, D), 1.0, 6.0, ((0, 128),)),
        "w_gate": scatter_about(arg_keys[1], (D, FF), D ** -0.5, 0.0625, ((1, 128),)),
        "w_up": scatter_about(arg_keys[2], (D, FF), D ** -0.5, 0.0625, ((1, 128),)),
        "w_down": scatter_about(arg_keys[3], (FF, D), FF ** -0.5, 0.03125, ((0, 8), (1, 16))),
        "a_gate": scatter_about(arg_keys[4], (D, ADAPTERS * R), D ** -0.5, 0.0625, ((1, 16),)),
        "a_up": scatter_about(arg_keys[5], (D, ADAPTERS * R), D ** -0.5, 0.0625, ((1, 16),)),
        "b_gate": scatter_about(arg_keys[6], (ADAPTERS * R, FF), R ** -0.5, 1.5, ((1, 128),)),
        "b_up": scatter_about(arg_keys[7], (ADAPTERS * R, FF), R ** -0.5, 1.5, ((1, 128),)),
        "a_down": scatter_about(arg_keys[8], (FF, ADAPTERS * R), FF ** -0.5, 0.03125, ((0, 128),)),
        "b_down": scatter_about(arg_keys[9], (ADAPTERS * R, D), R ** -0.5, 1.5, ((0, 16),)),
        "lengths": uneven(arg_keys[10], REQS, TOKENS, TOKENS // 4, 2).astype(jnp.int32),
        "request_adapter": with_ends(jax.random.randint(arg_keys[11], (REQS,), 0, ADAPTERS), jax.random.fold_in(arg_keys[11], 1), 0, ADAPTERS - 1).astype(jnp.int32),
        "placement": jax.random.permutation(arg_keys[12], ADAPTERS).astype(jnp.int32),
    }


def token_tables(lengths, request_adapter, placement, all_tokens):
    positions = jnp.arange(all_tokens, dtype=jnp.int32)
    request_ends = jnp.cumsum(lengths).astype(jnp.int32)
    request = jnp.sum((positions[:, None] >= request_ends[None, :]).astype(jnp.int32), axis=1)
    request_hot = request[:, None] == jnp.arange(lengths.shape[0], dtype=jnp.int32)[None, :]
    adapter = jnp.sum(jnp.where(request_hot, request_adapter[None, :], 0), axis=1).astype(jnp.int32)
    adapter_hot = adapter[:, None] == jnp.arange(placement.shape[0], dtype=jnp.int32)[None, :]
    slot_index = jnp.sum(jnp.where(adapter_hot, placement[None, :], 0), axis=1).astype(jnp.int32)
    return adapter_hot, slot_index


def pick_block(table, hot_rows, rank):
    shaped = table.reshape(table.shape[0], hot_rows.shape[1], rank)
    return jnp.sum(jnp.where(hot_rows[:, :, None], shaped, jnp.zeros_like(shaped)), axis=1)


def spread_block(low_rank, hot_rows):
    spread = jnp.where(hot_rows[:, :, None], low_rank[:, None, :], jnp.zeros_like(low_rank)[:, None, :])
    return spread.reshape(low_rank.shape[0], -1)


def reference(tokens_in, w_gate, w_up, w_down, a_gate, a_up, b_gate, b_up, a_down, b_down, lengths, request_adapter, placement):
    adapter_hot, slot_index = token_tables(lengths, request_adapter, placement, TOKENS)
    slot_hot = slot_index[:, None] == jnp.arange(ADAPTERS, dtype=jnp.int32)[None, :]
    shrunk_gate = pick_block(jnp.dot(tokens_in, a_gate, preferred_element_type=jnp.float32), slot_hot, R).astype(jnp.bfloat16)
    shrunk_up = pick_block(jnp.dot(tokens_in, a_up, preferred_element_type=jnp.float32), slot_hot, R).astype(jnp.bfloat16)
    gate_sum = jnp.dot(tokens_in, w_gate, preferred_element_type=jnp.float32) + jnp.dot(spread_block(shrunk_gate, adapter_hot), b_gate, preferred_element_type=jnp.float32)
    up_sum = jnp.dot(tokens_in, w_up, preferred_element_type=jnp.float32) + jnp.dot(spread_block(shrunk_up, adapter_hot), b_up, preferred_element_type=jnp.float32)
    hidden = (jax.nn.silu(gate_sum) * up_sum).astype(jnp.bfloat16)
    base_sum = jnp.dot(hidden, w_down, preferred_element_type=jnp.float32)
    low_rank = pick_block(jnp.dot(hidden, a_down, preferred_element_type=jnp.float32), adapter_hot, R).astype(jnp.bfloat16)
    delta_down = jnp.dot(spread_block(low_rank, slot_hot), b_down, preferred_element_type=jnp.float32).astype(jnp.bfloat16)
    return (base_sum + delta_down.astype(jnp.float32)).astype(jnp.bfloat16)
```

```python
import jax
import jax.numpy as jnp
from jax import lax
from jax.sharding import PartitionSpec as P

R = 16
N4 = 4

BF = jnp.bfloat16
F32 = jnp.float32


def shift(v, axis, s):
    if axis == "c":
        return lax.ppermute(v, "tensor", [(t, t ^ 1) for t in range(8)])
    if axis == "y":
        return lax.ppermute(v, "tensor", [(t, (t + 2 * s) % 8) for t in range(8)])
    if axis == "x":
        return lax.ppermute(v, "adapter", [(a, (a + 4 * s) % 16) for a in range(16)])
    return lax.ppermute(v, "adapter", [(a, a - a % 4 + (a + s) % 4) for a in range(16)])


def gather4(v, axis):
    return [v] + [shift(v, axis, s) for s in (1, 2, 3)]


def coords():
    t, a = lax.axis_index("tensor"), lax.axis_index("adapter")
    return {"y": t // 2, "c": t % 2, "x": a // 4, "z": a % 4}


def row_order(me, order):
    row = jnp.arange(512, dtype=jnp.int32)
    at = {}
    at["i"] = row % 4
    at[order[0]] = (me[order[0]] - row // 4 % 4) % 4
    at[order[1]] = (me[order[1]] - row // 16 % 4) % 4
    at[order[2]] = (me[order[2]] - row // 64 % 4) % 4
    at["c"] = (me["c"] + row // 256) % 2
    return (((at["y"] * 2 + at["c"]) * 4 + at["x"]) * 4 + at["z"]) * 4 + at["i"]


def block(v, at):
    return lax.dynamic_index_in_dim(v, at, 0, keepdims=False)


def local(
    tokens_in,
    w_gate,
    w_up,
    w_down,
    a_gate,
    a_up,
    b_gate,
    b_up,
    a_down,
    b_down,
    lengths,
    request_adapter,
    placement,
):
    me = coords()
    adp = lax.axis_index("adapter")
    ten = lax.axis_index("tensor")
    D = tokens_in.shape[1]
    positions = jnp.arange(512, dtype=jnp.int32)
    ends = jnp.cumsum(lengths)
    request = jnp.sum((positions[:, None] >= ends[None, :]).astype(jnp.int32), axis=1)
    request_hot = request[:, None] == jnp.arange(8, dtype=jnp.int32)[None, :]
    adapter_hot = request_adapter[:, None] == jnp.arange(128, dtype=jnp.int32)[None, :]
    slots = jnp.sum(jnp.where(adapter_hot, placement[None, :], 0), axis=1)
    slot_tok = jnp.sum(jnp.where(request_hot, slots[None, :], 0), axis=1)

    cuts = ((0, 2816), (2816, 5504), (5504, D))
    orders = (("x", "z", "y"), ("z", "y", "x"), ("y", "x", "z"))
    parts = [tokens_in[:, lo:hi] for lo, hi in cuts]
    for step in range(2):
        parts = [
            jnp.concatenate(gather4(v, order[step]), axis=0) for v, order in zip(parts, orders)
        ]
    last = [gather4(v, order[2]) for v, order in zip(parts, orders)]
    full = []
    for pieces in last:
        other = [shift(v, "c", 1) for v in pieces]
        full.append(jnp.concatenate(pieces + other, axis=0))

    tok = jnp.arange(512, dtype=jnp.int32)
    spread = [
        (row_order(me, order)[None, :] == tok[:, None]).astype(F32) for order in orders
    ]

    def product(w):
        cols = [
            jnp.dot(v, w[lo:hi], preferred_element_type=F32) for v, (lo, hi) in zip(full, cuts)
        ]
        return jnp.dot(
            jnp.concatenate(spread, axis=1),
            jnp.concatenate(cols, axis=0),
            precision=lax.Precision.HIGH,
            preferred_element_type=F32,
        )

    own_a = jnp.concatenate([a_gate, a_up], axis=1)
    shrunk = product(own_a)
    slot_cols = jnp.arange(256, dtype=jnp.int32) % 128 // R
    mine = (slot_tok[:, None] // 8 == adp) & (slot_tok[:, None] % 8 == slot_cols[None, :])
    picked = jnp.sum(jnp.where(mine, shrunk, 0.0).reshape(512, 2, 8, R), axis=2)
    picked = picked.reshape(512, 2 * R).astype(BF)

    slot_r = jnp.sum(jnp.where(jnp.arange(8) == ten, slots, 0))
    rows_b = lax.dynamic_slice_in_dim(b_down, slot_r % 8 * R, R, axis=0)
    rows_b = jnp.where(slot_r // 8 == adp, rows_b, jnp.zeros_like(rows_b))
    rows_b = rows_b.reshape(R, 4, 4, 512).transpose(2, 1, 0, 3)

    picked = picked.T
    rows_z = [block(rows_b, (me["z"] + s) % 4).reshape(64, 512) for s in range(4)]
    sent = [jnp.concatenate([picked, v], axis=0) for v in rows_z]
    got = [sent[0]] + [shift(sent[s], "z", s) for s in (1, 2, 3)]
    both = sum(v.astype(F32) for v in got).astype(BF)
    picked, rows_b = both[:32], both[32:].reshape(4, R, 512)
    sent = [
        jnp.concatenate([picked, block(rows_b, (me["x"] + s) % 4)], axis=0) for s in range(4)
    ]
    got = [sent[0]] + [shift(sent[s], "x", s) for s in (1, 2, 3)]
    both = sum(v.astype(F32) for v in got).astype(BF)
    shrunk_all, rows_b = both[:32].T, both[32:]
    rows_b = jnp.concatenate(gather4(rows_b, "y"), axis=0)
    rows_b = jnp.concatenate([rows_b, shift(rows_b, "c", 1)], axis=0)
    blk = jnp.arange(8, dtype=jnp.int32)
    blk_request = (me["y"] - blk % 4) % 4 * 2 + (me["c"] + blk // 4) % 2

    def spread_block(low, hot):
        return jnp.where(hot[:, :, None], low[:, None, :], jnp.zeros_like(low)[:, None, :]).reshape(
            low.shape[0], -1
        )

    def expand_rows(b):
        return jnp.concatenate(
            [lax.dynamic_slice_in_dim(b, request_adapter[q] * R, R, axis=0) for q in range(8)], axis=0
        )

    gate = product(w_gate) + jnp.dot(
        spread_block(shrunk_all[:, :R], request_hot), expand_rows(b_gate), preferred_element_type=F32
    )
    up = product(w_up) + jnp.dot(
        spread_block(shrunk_all[:, R:], request_hot), expand_rows(b_up), preferred_element_type=F32
    )
    hidden = (jax.nn.silu(gate) * up).astype(BF)

    pick = (
        (jnp.arange(2048, dtype=jnp.int32)[:, None] // R
         == jnp.repeat(request_adapter, R, total_repeat_length=128)[None, :])
        & (jnp.arange(2048, dtype=jnp.int32)[:, None] % R == jnp.arange(128, dtype=jnp.int32)[None, :] % R)
    ).astype(BF)
    down_cols = jnp.dot(a_down, pick, preferred_element_type=F32).astype(BF)
    low = jnp.dot(hidden, down_cols, preferred_element_type=F32).reshape(512, 8, R)
    low = jnp.sum(jnp.where(request_hot[:, :, None], low, 0.0), axis=1).astype(BF)
    hidden = jnp.concatenate([hidden, low, jnp.zeros((512, 16), BF)], axis=1)

    unit = jnp.concatenate(
        [jnp.zeros((224, 128), BF), jnp.eye(R, 128, dtype=BF), jnp.zeros((16, 128), BF)], axis=0
    )
    w_blocks = w_down.reshape(16, 224, 512)
    base = []
    for q, order in enumerate((("x", "z"), ("z", "x"))):
        h = hidden[q * 256 : q * 256 + 256]
        h = jnp.stack(gather4(h, order[0]), axis=0)
        pieces = gather4(h, order[1])
        acc = 0.0
        for r2 in range(4):
            for r1 in range(4):
                at = {order[0]: (me[order[0]] - r1) % 4, order[1]: (me[order[1]] - r2) % 4}
                w = block(w_blocks, at["x"] * 4 + at["z"])
                w = jnp.concatenate([w, jnp.zeros((32, 512), BF)], axis=0)
                w = jnp.concatenate([w, unit], axis=1)
                acc = acc + jnp.dot(pieces[r2][r1], w, preferred_element_type=F32)
        base.append(acc)
    base = jnp.concatenate(base, axis=0)
    hot_blk = request[:, None] == blk_request[None, :]
    delta = jnp.dot(
        spread_block(base[:, 512 : 512 + R].astype(BF), hot_blk), rows_b, preferred_element_type=F32
    )
    out = (base[:, :512] + delta).reshape(4, 2, 64, 512)

    out = out.transpose(1, 0, 2, 3)
    got = shift(block(out, 1 - me["c"]).astype(BF), "c", 1)
    out = block(out, me["c"]) + got.astype(F32)
    acc = block(out, me["y"])
    for s in (1, 2, 3):
        acc = acc + shift(block(out, (me["y"] + s) % 4).astype(BF), "y", s).astype(F32)
    mixed = acc.astype(BF)

    mixed = mixed.reshape(4, 16, 512)
    got = [block(mixed, me["x"])] + [shift(block(mixed, (me["x"] + s) % 4), "x", s) for s in (1, 2, 3)]
    mixed = jnp.stack(got, axis=0).reshape(4, 4, 4, 512).transpose(1, 0, 2, 3)
    got = [block(mixed, me["z"])] + [shift(block(mixed, (me["z"] + s) % 4), "z", s) for s in (1, 2, 3)]
    mixed = jnp.stack(got, axis=1)
    mixed = jnp.take(mixed, (me["x"] - jnp.arange(4)) % 4, axis=0)
    mixed = jnp.take(mixed, (me["z"] - jnp.arange(4)) % 4, axis=1)
    return mixed.transpose(2, 0, 1, 3).reshape(4, D)


def solution(mesh):
    in_specs = (
        P(("tensor", "adapter"), None),
        P(None, ("tensor", "adapter")),
        P(None, ("tensor", "adapter")),
        P("tensor", "adapter"),
        P(None, "adapter"),
        P(None, "adapter"),
        P(None, ("tensor", "adapter")),
        P(None, ("tensor", "adapter")),
        P(("tensor", "adapter"), None),
        P("adapter", None),
        P(),
        P(),
        P(),
    )
    out_specs = P(("tensor", "adapter"), None)
    return jax.shard_map(local, mesh=mesh, in_specs=in_specs, out_specs=out_specs, check_vma=False)
```

```python
import jax
import jax.numpy as jnp
from jax import lax
from jax.experimental import pallas as pl
from jax.experimental.pallas import tpu as pltpu
from jax.sharding import PartitionSpec as P

R = 16
N4 = 4

BF = jnp.bfloat16
F32 = jnp.float32


def shift(v, axis, s):
    if axis == "c":
        return lax.ppermute(v, "tensor", [(t, t ^ 1) for t in range(8)])
    if axis == "y":
        return lax.ppermute(v, "tensor", [(t, (t + 2 * s) % 8) for t in range(8)])
    if axis == "x":
        return lax.ppermute(v, "adapter", [(a, (a + 4 * s) % 16) for a in range(16)])
    return lax.ppermute(v, "adapter", [(a, a - a % 4 + (a + s) % 4) for a in range(16)])


def gather4(v, axis):
    return [v] + [shift(v, axis, s) for s in (1, 2, 3)]


def coords():
    t, a = lax.axis_index("tensor"), lax.axis_index("adapter")
    return {"y": t >> 1, "c": t & 1, "x": a >> 2, "z": a & 3}


KB = 1024


def products_kernel(*refs):
    p, q = refs[:8], refs[8:16]
    wg, wu, ag, au, gate, up, shrunk = refs[16:]
    k = pl.program_id(0)
    steps = pl.num_programs(0) // 2

    @pl.when(k == 0)
    def _():
        gate[...] = jnp.zeros_like(gate)
        up[...] = jnp.zeros_like(up)
        shrunk[...] = jnp.zeros_like(shrunk)

    def add(rows):
        last = (((1,), (1,)), ((), ()))
        gate[...] += lax.dot_general(rows, wg[...], last, preferred_element_type=F32)
        up[...] += lax.dot_general(rows, wu[...], last, preferred_element_type=F32)
        a = jnp.concatenate([ag[...], au[...]], axis=1)
        shrunk[...] += jnp.dot(rows, a, preferred_element_type=F32)

    @pl.when(k < steps)
    def _():
        add(jnp.concatenate([v[...] for v in p], axis=0))

    @pl.when(k >= steps)
    def _():
        add(
            jnp.concatenate(
                [
                    q[c * 4 + x][y * 16 : y * 16 + 16, :]
                    for c in range(2)
                    for y in range(4)
                    for x in range(4)
                ],
                axis=0,
            )
        )


def products(p, q, w_gate, w_up, a_gate, a_up):
    half = p[0].shape[1]
    steps = half // KB
    rows = [pl.BlockSpec((64, KB), lambda k: (0, jnp.minimum(k, steps - 1)))] * 8
    rows += [pl.BlockSpec((64, KB), lambda k: (0, jnp.maximum(k - steps, 0)))] * 8
    units = w_gate.shape[1]
    cols = [pl.BlockSpec((units, KB), lambda k: (0, k))] * 2
    cols += [pl.BlockSpec((KB, 128), lambda k: (k, 0))] * 2
    return pl.pallas_call(
        products_kernel,
        grid=(2 * steps,),
        in_specs=rows + cols,
        out_specs=[
            pl.BlockSpec((512, units), lambda k: (0, 0)),
            pl.BlockSpec((512, units), lambda k: (0, 0)),
            pl.BlockSpec((512, 256), lambda k: (0, 0)),
        ],
        out_shape=[
            jax.ShapeDtypeStruct((512, units), F32),
            jax.ShapeDtypeStruct((512, units), F32),
            jax.ShapeDtypeStruct((512, 256), F32),
        ],
        compiler_params=pltpu.CompilerParams(vmem_limit_bytes=40 << 20),
        name="products",
    )(*p, *q, w_gate.T, w_up.T, a_gate, a_up)


def row_order(me, order):
    row = jnp.arange(512, dtype=jnp.int32)
    at = {}
    at[order[0]] = (me[order[0]] - (row >> 2)) & 3
    at[order[1]] = (me[order[1]] - (row >> 4)) & 3
    at[order[2]] = (me[order[2]] - (row >> 6)) & 3
    at["c"] = (me["c"] + (row >> 8)) & 1
    return (at["y"] << 7) | (at["c"] << 6) | (at["x"] << 4) | (at["z"] << 2) | (row & 3)


def block(v, at):
    return lax.dynamic_index_in_dim(v, at, 0, keepdims=False)


def local(
    tokens_in,
    w_gate,
    w_up,
    w_down,
    a_gate,
    a_up,
    b_gate,
    b_up,
    a_down,
    b_down,
    lengths,
    request_adapter,
    placement,
):
    me = coords()
    D = tokens_in.shape[1]

    half = D // 2
    v = jnp.concatenate(gather4(tokens_in, "z"), axis=0)
    p = jnp.concatenate(gather4(v[:, :half], "x"), axis=0)
    q = jnp.concatenate(gather4(v[:, half:], "y"), axis=0)
    p, q, lengths, request_adapter, placement, ten, adp = lax.optimization_barrier(
        (p, q, lengths, request_adapter, placement, lax.axis_index("tensor"), lax.axis_index("adapter"))
    )
    me = {"y": ten >> 1, "c": ten & 1, "x": adp >> 2, "z": adp & 3}
    p, q = gather4(p, "y"), gather4(q, "x")
    p = p + [shift(v, "c", 1) for v in p]
    q = q + [shift(v, "c", 1) for v in q]

    positions = jnp.arange(512, dtype=jnp.int32)
    ends = jnp.sum(
        jnp.where(jnp.arange(8)[:, None] <= jnp.arange(8)[None, :], lengths[:, None], 0), axis=0
    )
    request = jnp.sum((positions[:, None] >= ends[None, :]).astype(jnp.int32), axis=1)
    adapter_hot = request_adapter[:, None] == jnp.arange(128, dtype=jnp.int32)[None, :]
    slots = jnp.sum(jnp.where(adapter_hot, placement[None, :], 0), axis=1)
    request_hot = request[:, None] == jnp.arange(8, dtype=jnp.int32)[None, :]

    slot_r = jnp.sum(jnp.where(jnp.arange(8) == ten, slots, 0))
    rows_b = lax.dynamic_slice_in_dim(b_down, (slot_r & 7) * R, R, axis=0)
    rows_b = jnp.where(slot_r >> 3 == adp, rows_b, jnp.zeros_like(rows_b))
    rows_b = rows_b.reshape(R, 4, 4, 512).transpose(2, 1, 0, 3)
    for axis in ("z", "x"):
        got = [block(rows_b, me[axis])]
        got += [shift(block(rows_b, (me[axis] + s) & 3), axis, s) for s in (1, 2, 3)]
        rows_b = sum(v.astype(F32) for v in got).astype(BF)
    rows_b = jnp.concatenate(gather4(rows_b, "y"), axis=0)
    rows_b = jnp.concatenate([rows_b, shift(rows_b, "c", 1)], axis=0)
    blk = jnp.arange(8, dtype=jnp.int32)
    blk_request = ((me["y"] - blk) & 3) << 1 | (me["c"] + (blk >> 2)) & 1

    wide = jnp.arange(2048, dtype=jnp.int32)
    rank = jnp.arange(128, dtype=jnp.int32)
    own_adapter = jnp.sum(
        jnp.where((rank >> 4)[:, None] == jnp.arange(8)[None, :], request_adapter[None, :], 0), axis=1
    )
    pick = (wide[:, None] == ((own_adapter << 4) | (rank & 15))[None, :]).astype(BF)
    take = (((0,), (0,)), ((), ()))
    gate_rows = lax.dot_general(pick, b_gate, take, preferred_element_type=F32).astype(BF)
    up_rows = lax.dot_general(pick, b_up, take, preferred_element_type=F32).astype(BF)
    down_cols = jnp.dot(a_down, pick, preferred_element_type=F32).astype(BF)

    unit = jnp.concatenate(
        [jnp.zeros((224, 128), BF), jnp.eye(R, 128, dtype=BF), jnp.zeros((16, 128), BF)], axis=0
    )
    w_blocks = w_down.reshape(16, 224, 512)

    gate, up, shrunk = products(p, q, w_gate, w_up, a_gate, a_up)

    tok = jnp.arange(512, dtype=jnp.int32)
    held = row_order(me, ("z", "x", "y"))
    put = (held[None, :] == tok[:, None]).astype(BF)
    get = (held[:, None] == tok[None, :]).astype(BF)
    row_hot = jnp.dot(get, request_hot.astype(BF), preferred_element_type=F32) > 0.5
    row_slot = jnp.sum(jnp.where(row_hot, slots[None, :], 0), axis=1)

    slot_cols = jnp.arange(256, dtype=jnp.int32) % 128 // R
    mine = (row_slot[:, None] >> 3 == adp) & (row_slot[:, None] & 7 == slot_cols[None, :])
    fold = (jnp.arange(256)[:, None] % R + jnp.arange(256)[:, None] // 128 * R
            == jnp.arange(2 * R)[None, :]).astype(BF)
    picked = jnp.where(mine, shrunk, 0.0).astype(BF)
    picked = jnp.dot(picked, fold, preferred_element_type=F32).astype(BF)
    picked = lax.dot_general(
        picked, put, (((0,), (1,)), ((), ())), preferred_element_type=F32
    ).astype(BF)

    for axis in ("z", "x"):
        picked = sum(v.astype(F32) for v in gather4(picked, axis)).astype(BF)
    shrunk_all = lax.dot_general(
        get, picked, (((1,), (1,)), ((), ())), preferred_element_type=F32
    ).astype(BF)

    def spread_block(low, hot):
        return jnp.where(hot[:, :, None], low[:, None, :], jnp.zeros_like(low)[:, None, :]).reshape(
            low.shape[0], -1
        )

    gate = gate + jnp.dot(
        spread_block(shrunk_all[:, :R], row_hot), gate_rows, preferred_element_type=F32
    )
    up = up + jnp.dot(
        spread_block(shrunk_all[:, R:], row_hot), up_rows, preferred_element_type=F32
    )
    hidden = (jax.nn.silu(gate) * up).astype(BF)

    low = jnp.dot(hidden, down_cols, preferred_element_type=F32).reshape(512, 8, R)
    low = jnp.sum(jnp.where(row_hot[:, :, None], low, 0.0), axis=1).astype(BF)
    hidden = jnp.concatenate([hidden, low, jnp.zeros((512, 16), BF)], axis=1)
    hidden = jnp.dot(put, hidden, preferred_element_type=F32).astype(BF)

    base = []
    for q, order in enumerate((("x", "z"), ("z", "x"))):
        h = hidden[q * 256 : q * 256 + 256]
        h = jnp.stack(gather4(h, order[0]), axis=0)
        pieces = gather4(h, order[1])
        acc = 0.0
        for r2 in range(4):
            for r1 in range(4):
                at = {order[0]: (me[order[0]] - r1) & 3, order[1]: (me[order[1]] - r2) & 3}
                w = block(w_blocks, at["x"] << 2 | at["z"])
                w = jnp.concatenate([w, jnp.zeros((32, 512), BF)], axis=0)
                w = jnp.concatenate([w, unit], axis=1)
                acc = acc + jnp.dot(pieces[r2][r1], w, preferred_element_type=F32)
        base.append(acc)
    base = jnp.concatenate(base, axis=0)
    hot_blk = request[:, None] == blk_request[None, :]
    delta = jnp.dot(
        spread_block(base[:, 512 : 512 + R].astype(BF), hot_blk), rows_b, preferred_element_type=F32
    )
    out = (base[:, :512] + delta).astype(BF).reshape(128, 4, 512)

    got = lax.all_to_all(out, ("tensor", "adapter"), 0, 0, tiled=True)
    mixed = jnp.sum(got.reshape(8, 16, 4, 512).astype(F32), axis=0).astype(BF)
    return mixed.transpose(1, 0, 2).reshape(4, D)


def solution(mesh):
    in_specs = (
        P(("tensor", "adapter"), None),
        P(None, ("tensor", "adapter")),
        P(None, ("tensor", "adapter")),
        P("tensor", "adapter"),
        P(None, "adapter"),
        P(None, "adapter"),
        P(None, ("tensor", "adapter")),
        P(None, ("tensor", "adapter")),
        P(("tensor", "adapter"), None),
        P("adapter", None),
        P(),
        P(),
        P(),
    )
    out_specs = P(("tensor", "adapter"), None)
    return jax.shard_map(local, mesh=mesh, in_specs=in_specs, out_specs=out_specs, check_vma=False)
```

```python
import jax
import jax.numpy as jnp
from jax import lax
from jax.experimental import pallas as pl
from jax.experimental.pallas import tpu as pltpu
from jax.sharding import PartitionSpec as P

R = 16
N4 = 4

BF = jnp.bfloat16
F32 = jnp.float32


def shift(v, axis, s):
    if axis == "c":
        return lax.ppermute(v, "tensor", [(t, t ^ 1) for t in range(8)])
    if axis == "y":
        return lax.ppermute(v, "tensor", [(t, (t + 2 * s) % 8) for t in range(8)])
    if axis == "x":
        return lax.ppermute(v, "adapter", [(a, (a + 4 * s) % 16) for a in range(16)])
    return lax.ppermute(v, "adapter", [(a, a - a % 4 + (a + s) % 4) for a in range(16)])


def gather4(v, axis):
    return [v] + [shift(v, axis, s) for s in (1, 2, 3)]


def ring4(v, axis):
    n = v.shape[0] // 2
    near, far = shift(v, axis, 1), shift(v, axis, 3)
    return [v, near, shift(near[:n], axis, 1), shift(far[n:], axis, 3), far]


def coords():
    t, a = lax.axis_index("tensor"), lax.axis_index("adapter")
    return {"y": t >> 1, "c": t & 1, "x": a >> 2, "z": a & 3}


KB = 1024


def products_kernel(*refs):
    p, q = refs[:10], refs[10:20]
    wg, wu, ag, au, gate, up, shrunk = refs[20:]
    k = pl.program_id(0)
    steps = pl.num_programs(0) // 2

    @pl.when(k == 0)
    def _():
        gate[...] = jnp.zeros_like(gate)
        up[...] = jnp.zeros_like(up)
        shrunk[...] = jnp.zeros_like(shrunk)

    def add(rows):
        last = (((1,), (1,)), ((), ()))
        gate[...] += lax.dot_general(rows, wg[...], last, preferred_element_type=F32)
        up[...] += lax.dot_general(rows, wu[...], last, preferred_element_type=F32)
        a = jnp.concatenate([ag[...], au[...]], axis=1)
        shrunk[...] += jnp.dot(rows, a, preferred_element_type=F32)

    @pl.when(k < steps)
    def _():
        add(jnp.concatenate([v[...] for v in p], axis=0))

    @pl.when(k >= steps)
    def _():
        blocks = []
        for c in range(2):
            for y in range(4):
                for x in range(4):
                    at = y * 16
                    if x == 2 and y > 1:
                        at -= 32
                    ref = q[c * 5 + (x if x < 2 else 4 if x == 3 else 2 + y // 2)]
                    blocks.append(ref[at : at + 16, :])
        add(jnp.concatenate(blocks, axis=0))


def products(p, q, w_gate, w_up, a_gate, a_up):
    half = p[0].shape[1]
    steps = half // KB
    rows = [pl.BlockSpec((v.shape[0], KB), lambda k: (0, jnp.minimum(k, steps - 1))) for v in p]
    rows += [pl.BlockSpec((v.shape[0], KB), lambda k: (0, jnp.maximum(k - steps, 0))) for v in q]
    units = w_gate.shape[1]
    cols = [pl.BlockSpec((units, KB), lambda k: (0, k))] * 2
    cols += [pl.BlockSpec((KB, 128), lambda k: (k, 0))] * 2
    return pl.pallas_call(
        products_kernel,
        grid=(2 * steps,),
        in_specs=rows + cols,
        out_specs=[
            pl.BlockSpec((512, units), lambda k: (0, 0)),
            pl.BlockSpec((512, units), lambda k: (0, 0)),
            pl.BlockSpec((512, 256), lambda k: (0, 0)),
        ],
        out_shape=[
            jax.ShapeDtypeStruct((512, units), F32),
            jax.ShapeDtypeStruct((512, units), F32),
            jax.ShapeDtypeStruct((512, 256), F32),
        ],
        compiler_params=pltpu.CompilerParams(vmem_limit_bytes=40 << 20),
        name="products",
    )(*p, *q, w_gate.T, w_up.T, a_gate, a_up)


def row_order(me, order):
    row = jnp.arange(512, dtype=jnp.int32)
    at = {}
    at[order[0]] = (me[order[0]] - (row >> 2)) & 3
    at[order[1]] = (me[order[1]] - (row >> 4)) & 3
    at[order[2]] = (me[order[2]] - (row >> 6)) & 3
    at["c"] = (me["c"] + (row >> 8)) & 1
    return (at["y"] << 7) | (at["c"] << 6) | (at["x"] << 4) | (at["z"] << 2) | (row & 3)


def block(v, at):
    return lax.dynamic_index_in_dim(v, at, 0, keepdims=False)


def local(
    tokens_in,
    w_gate,
    w_up,
    w_down,
    a_gate,
    a_up,
    b_gate,
    b_up,
    a_down,
    b_down,
    lengths,
    request_adapter,
    placement,
):
    me = coords()
    D = tokens_in.shape[1]

    half = D // 2
    v = jnp.concatenate(gather4(tokens_in, "z"), axis=0)
    p = jnp.concatenate(gather4(v[:, :half], "x"), axis=0)
    q = jnp.concatenate(gather4(v[:, half:], "y"), axis=0)
    p, q, lengths, request_adapter, placement, ten, adp = lax.optimization_barrier(
        (p, q, lengths, request_adapter, placement, lax.axis_index("tensor"), lax.axis_index("adapter"))
    )
    me = {"y": ten >> 1, "c": ten & 1, "x": adp >> 2, "z": adp & 3}
    p, q = ring4(p, "y"), ring4(q, "x")
    p = p + [shift(v, "c", 1) for v in p]
    q = q + [shift(v, "c", 1) for v in q]

    positions = jnp.arange(512, dtype=jnp.int32)
    ends = jnp.sum(
        jnp.where(jnp.arange(8)[:, None] <= jnp.arange(8)[None, :], lengths[:, None], 0), axis=0
    )
    request = jnp.sum((positions[:, None] >= ends[None, :]).astype(jnp.int32), axis=1)
    adapter_hot = request_adapter[:, None] == jnp.arange(128, dtype=jnp.int32)[None, :]
    slots = jnp.sum(jnp.where(adapter_hot, placement[None, :], 0), axis=1)
    request_hot = request[:, None] == jnp.arange(8, dtype=jnp.int32)[None, :]

    slot_r = jnp.sum(jnp.where(jnp.arange(8) == ten, slots, 0))
    rows_b = lax.dynamic_slice_in_dim(b_down, (slot_r & 7) * R, R, axis=0)
    rows_b = jnp.where(slot_r >> 3 == adp, rows_b, jnp.zeros_like(rows_b))
    rows_b = rows_b.reshape(R, 4, 4, 512).transpose(2, 1, 0, 3)
    got = [block(rows_b, me["z"])]
    got += [shift(block(rows_b, (me["z"] + s) & 3), "z", s) for s in (1, 2, 3)]
    rows_b = sum(v.astype(F32) for v in got).astype(BF)
    blk = jnp.arange(8, dtype=jnp.int32)
    blk_request = ((me["y"] - blk) & 3) << 1 | (me["c"] + (blk >> 2)) & 1

    wide = jnp.arange(2048, dtype=jnp.int32)
    rank = jnp.arange(128, dtype=jnp.int32)
    own_adapter = jnp.sum(
        jnp.where((rank >> 4)[:, None] == jnp.arange(8)[None, :], request_adapter[None, :], 0), axis=1
    )
    pick = (wide[:, None] == ((own_adapter << 4) | (rank & 15))[None, :]).astype(BF)
    take = (((0,), (0,)), ((), ()))
    gate_rows = lax.dot_general(pick, b_gate, take, preferred_element_type=F32).astype(BF)
    up_rows = lax.dot_general(pick, b_up, take, preferred_element_type=F32).astype(BF)
    down_cols = jnp.dot(a_down, pick, preferred_element_type=F32).astype(BF)

    unit = jnp.concatenate(
        [jnp.zeros((224, 128), BF), jnp.eye(R, 128, dtype=BF), jnp.zeros((16, 128), BF)], axis=0
    )
    w_blocks = w_down.reshape(16, 224, 512)

    gate, up, shrunk = products(p, q, w_gate, w_up, a_gate, a_up)

    tok = jnp.arange(512, dtype=jnp.int32)
    held = row_order(me, ("z", "x", "y"))
    put = (held[None, :] == tok[:, None]).astype(BF)
    get = (held[:, None] == tok[None, :]).astype(BF)
    row_hot = jnp.dot(get, request_hot.astype(BF), preferred_element_type=F32) > 0.5
    row_slot = jnp.sum(jnp.where(row_hot, slots[None, :], 0), axis=1)

    slot_cols = jnp.arange(256, dtype=jnp.int32) % 128 // R
    mine = (row_slot[:, None] >> 3 == adp) & (row_slot[:, None] & 7 == slot_cols[None, :])
    fold = (jnp.arange(256)[:, None] % R + jnp.arange(256)[:, None] // 128 * R
            == jnp.arange(2 * R)[None, :]).astype(BF)
    picked = jnp.where(mine, shrunk, 0.0).astype(BF)
    picked = jnp.dot(picked, fold, preferred_element_type=F32).astype(BF)
    picked = lax.dot_general(
        picked, put, (((0,), (1,)), ((), ())), preferred_element_type=F32
    ).astype(BF)

    picked = sum(v.astype(F32) for v in gather4(picked, "z")).astype(BF)
    sent = [
        jnp.concatenate([picked, block(rows_b, (me["x"] + s) & 3)], axis=0) for s in range(4)
    ]
    got = [sent[0]] + [shift(sent[s], "x", s) for s in (1, 2, 3)]
    both = sum(v.astype(F32) for v in got).astype(BF)
    picked, rows_b = both[: 2 * R], both[2 * R :]
    shrunk_all = lax.dot_general(
        get, picked, (((1,), (1,)), ((), ())), preferred_element_type=F32
    ).astype(BF)

    def spread_block(low, hot):
        return jnp.where(hot[:, :, None], low[:, None, :], jnp.zeros_like(low)[:, None, :]).reshape(
            low.shape[0], -1
        )

    gate = gate + jnp.dot(
        spread_block(shrunk_all[:, :R], row_hot), gate_rows, preferred_element_type=F32
    )
    up = up + jnp.dot(
        spread_block(shrunk_all[:, R:], row_hot), up_rows, preferred_element_type=F32
    )
    hidden = (jax.nn.silu(gate) * up).astype(BF)

    low = jnp.dot(hidden, down_cols, preferred_element_type=F32).reshape(512, 8, R)
    low = jnp.sum(jnp.where(row_hot[:, :, None], low, 0.0), axis=1).astype(BF)
    hidden = jnp.concatenate([hidden, low, jnp.zeros((512, 16), BF)], axis=1)
    hidden = jnp.dot(put, hidden, preferred_element_type=F32).astype(BF)

    ways = (("x", "z"), ("z", "x"))
    first = [
        jnp.stack(gather4(hidden[i * 256 : i * 256 + 256], way[0]), axis=0)
        for i, way in enumerate(ways)
    ]
    *first, rows_b = lax.optimization_barrier((*first, rows_b))
    pieces = [ring4(h, way[1]) for h, way in zip(first, ways)]
    rows_b = jnp.concatenate(gather4(rows_b, "y"), axis=0)
    rows_b = jnp.concatenate([rows_b, shift(rows_b, "c", 1)], axis=0)
    base = []
    for (own, near, low_half, high_half, far), way in zip(pieces, ways):
        acc = 0.0
        for r2, piece in ((0, own), (1, near), (3, far), (2, low_half), (2, high_half)):
            for i in range(piece.shape[0]):
                r1 = i + 2 if piece is high_half else i
                at = {way[0]: (me[way[0]] - r1) & 3, way[1]: (me[way[1]] - r2) & 3}
                w = block(w_blocks, at["x"] << 2 | at["z"])
                w = jnp.concatenate([w, jnp.zeros((32, 512), BF)], axis=0)
                w = jnp.concatenate([w, unit], axis=1)
                acc = acc + jnp.dot(piece[i], w, preferred_element_type=F32)
        base.append(acc)
    base = jnp.concatenate(base, axis=0)
    hot_blk = request[:, None] == blk_request[None, :]
    delta = jnp.dot(
        spread_block(base[:, 512 : 512 + R].astype(BF), hot_blk), rows_b, preferred_element_type=F32
    )
    out = (base[:, :512] + delta).astype(BF).reshape(128, 4, 512)

    got = lax.all_to_all(out, ("tensor", "adapter"), 0, 0, tiled=True)
    mixed = jnp.sum(got.reshape(8, 16, 4, 512).astype(F32), axis=0).astype(BF)
    return mixed.transpose(1, 0, 2).reshape(4, D)


def solution(mesh):
    in_specs = (
        P(("tensor", "adapter"), None),
        P(None, ("tensor", "adapter")),
        P(None, ("tensor", "adapter")),
        P("tensor", "adapter"),
        P(None, "adapter"),
        P(None, "adapter"),
        P(None, ("tensor", "adapter")),
        P(None, ("tensor", "adapter")),
        P(("tensor", "adapter"), None),
        P("adapter", None),
        P(),
        P(),
        P(),
    )
    out_specs = P(("tensor", "adapter"), None)
    return jax.shard_map(local, mesh=mesh, in_specs=in_specs, out_specs=out_specs, check_vma=False)
```

```python
import jax
import jax.numpy as jnp
from jax import lax
from jax.experimental import pallas as pl
from jax.experimental.pallas import tpu as pltpu
from jax.sharding import PartitionSpec as P

R = 16
N4 = 4

BF = jnp.bfloat16
F32 = jnp.float32


def shift(v, axis, s):
    if axis == "c":
        return lax.ppermute(v, "tensor", [(t, t ^ 1) for t in range(8)])
    if axis == "y":
        return lax.ppermute(v, "tensor", [(t, (t + 2 * s) % 8) for t in range(8)])
    if axis == "x":
        return lax.ppermute(v, "adapter", [(a, (a + 4 * s) % 16) for a in range(16)])
    return lax.ppermute(v, "adapter", [(a, a - a % 4 + (a + s) % 4) for a in range(16)])


def gather4(v, axis):
    return [v] + [shift(v, axis, s) for s in (1, 2, 3)]


def ring4(v, axis):
    n = v.shape[0] // 2
    near, far = shift(v, axis, 1), shift(v, axis, 3)
    return [v, near, shift(near[:n], axis, 1), shift(far[n:], axis, 3), far]


def coords():
    t, a = lax.axis_index("tensor"), lax.axis_index("adapter")
    return {"y": t >> 1, "c": t & 1, "x": a >> 2, "z": a & 3}


KB = 1024


def products_kernel(*refs):
    p, q = refs[:10], refs[10:20]
    wg, wu, ag, au, own_slot, get, gate, up, picked, shrunk = refs[20:]
    k = pl.program_id(0)
    steps = pl.num_programs(0) // 2

    @pl.when(k == 0)
    def _():
        gate[...] = jnp.zeros_like(gate)
        up[...] = jnp.zeros_like(up)
        shrunk[...] = jnp.zeros_like(shrunk)

    def add(rows):
        last = (((1,), (1,)), ((), ()))
        gate[...] += lax.dot_general(rows, wg[...], last, preferred_element_type=F32)
        up[...] += lax.dot_general(rows, wu[...], last, preferred_element_type=F32)
        a = jnp.concatenate([ag[...], au[...]], axis=1)
        shrunk[...] += jnp.dot(rows, a, preferred_element_type=F32)

    @pl.when(k < steps)
    def _():
        add(jnp.concatenate([v[...] for v in p], axis=0))

    @pl.when(k >= steps)
    def _():
        blocks = []
        for c in range(2):
            for y in range(4):
                for x in range(4):
                    at = y * 16
                    if x == 2 and y > 1:
                        at -= 32
                    ref = q[c * 5 + (x if x < 2 else 4 if x == 3 else 2 + y // 2)]
                    blocks.append(ref[at : at + 16, :])
        add(jnp.concatenate(blocks, axis=0))

    @pl.when(k == pl.num_programs(0) - 1)
    def _():
        lane = lax.broadcasted_iota(jnp.int32, (512, 256), 1)
        kept = jnp.where(own_slot[...] == (lane & 127) >> 4, shrunk[...], 0.0).astype(BF)
        fold = one_hot((256, 128), lambda r, c: (r & 15 | (r >> 7) << 4) == c)
        kept = jnp.dot(kept, fold, preferred_element_type=F32)
        kept = kept.T.astype(BF)[:32]
        picked[...] = jnp.dot(kept, get[...], preferred_element_type=F32).astype(BF)


def one_hot(shape, test):
    r = lax.broadcasted_iota(jnp.int32, shape, 0)
    c = lax.broadcasted_iota(jnp.int32, shape, 1)
    return jnp.where(test(r, c), 1.0, 0.0).astype(BF)


def hidden_kernel(gate, up, shrunk, get, row_request, gate_rows, up_rows, down_cols, out):
    last = (((1,), (1,)), ((), ()))
    low = lax.dot_general(get[...], shrunk[...], last, preferred_element_type=F32).astype(BF)
    wide = one_hot((2 * R, 256), lambda r, c: (c & 15 | (c >> 7) << 4) == r)
    low = jnp.dot(low, wide, preferred_element_type=F32)
    lane = lax.broadcasted_iota(jnp.int32, (512, 256), 1)
    hot = row_request[...] == (lane & 127) >> 4
    low = jnp.where(hot, low, 0.0).astype(BF)
    g = gate[...] + jnp.dot(low[:, :128], gate_rows[...], preferred_element_type=F32)
    u = up[...] + jnp.dot(low[:, 128:], up_rows[...], preferred_element_type=F32)
    hidden = (g / (1.0 + jnp.exp(-g)) * u).astype(BF)
    down = jnp.dot(hidden, down_cols[...], preferred_element_type=F32)
    down = jnp.where(hot[:, :128], down, 0.0).astype(BF)
    units = hidden.shape[1]
    place = one_hot((units, 256), lambda r, c: r == c)
    after = one_hot((128, 256), lambda r, c: (r & 15) + units == c)
    both = jnp.dot(hidden, place, preferred_element_type=F32)
    both = (both + jnp.dot(down, after, preferred_element_type=F32)).astype(BF)
    first = (((0,), (0,)), ((), ()))
    out[...] = lax.dot_general(get[...], both, first, preferred_element_type=F32).astype(BF)


def hidden_of(*args):
    return pl.pallas_call(
        hidden_kernel,
        out_shape=jax.ShapeDtypeStruct((512, 256), BF),
        compiler_params=pltpu.CompilerParams(vmem_limit_bytes=32 << 20),
        name="hidden",
    )(*args)


def products(p, q, w_gate, w_up, a_gate, a_up, own_slot, get):
    half = p[0].shape[1]
    steps = half // KB
    rows = [pl.BlockSpec((v.shape[0], KB), lambda k: (0, jnp.minimum(k, steps - 1))) for v in p]
    rows += [pl.BlockSpec((v.shape[0], KB), lambda k: (0, jnp.maximum(k - steps, 0))) for v in q]
    units = w_gate.shape[1]
    cols = [pl.BlockSpec((units, KB), lambda k: (0, k))] * 2
    cols += [pl.BlockSpec((KB, 128), lambda k: (k, 0))] * 2
    cols += [pl.BlockSpec((512, 1), lambda k: (0, 0)), pl.BlockSpec((512, 512), lambda k: (0, 0))]
    return pl.pallas_call(
        products_kernel,
        grid=(2 * steps,),
        in_specs=rows + cols,
        out_specs=[
            pl.BlockSpec((512, units), lambda k: (0, 0)),
            pl.BlockSpec((512, units), lambda k: (0, 0)),
            pl.BlockSpec((2 * R, 512), lambda k: (0, 0)),
        ],
        out_shape=[
            jax.ShapeDtypeStruct((512, units), F32),
            jax.ShapeDtypeStruct((512, units), F32),
            jax.ShapeDtypeStruct((2 * R, 512), BF),
        ],
        scratch_shapes=[pltpu.VMEM((512, 256), F32)],
        compiler_params=pltpu.CompilerParams(vmem_limit_bytes=40 << 20),
        name="products",
    )(*p, *q, w_gate.T, w_up.T, a_gate, a_up, own_slot, get)


def row_order(me, order):
    row = jnp.arange(512, dtype=jnp.int32)
    at = {}
    at[order[0]] = (me[order[0]] - (row >> 2)) & 3
    at[order[1]] = (me[order[1]] - (row >> 4)) & 3
    at[order[2]] = (me[order[2]] - (row >> 6)) & 3
    at["c"] = (me["c"] + (row >> 8)) & 1
    return (at["y"] << 7) | (at["c"] << 6) | (at["x"] << 4) | (at["z"] << 2) | (row & 3)


def block(v, at):
    return lax.dynamic_index_in_dim(v, at, 0, keepdims=False)


def local(
    tokens_in,
    w_gate,
    w_up,
    w_down,
    a_gate,
    a_up,
    b_gate,
    b_up,
    a_down,
    b_down,
    lengths,
    request_adapter,
    placement,
):
    me = coords()
    D = tokens_in.shape[1]

    half = D // 2
    v = jnp.concatenate(gather4(tokens_in, "z"), axis=0)
    p = jnp.concatenate(gather4(v[:, :half], "x"), axis=0)
    q = jnp.concatenate(gather4(v[:, half:], "y"), axis=0)
    p, q, lengths, request_adapter, placement, ten, adp = lax.optimization_barrier(
        (p, q, lengths, request_adapter, placement, lax.axis_index("tensor"), lax.axis_index("adapter"))
    )
    me = {"y": ten >> 1, "c": ten & 1, "x": adp >> 2, "z": adp & 3}
    p, q = ring4(p, "y"), ring4(q, "x")
    p = p + [shift(v, "c", 1) for v in p]
    q = q + [shift(v, "c", 1) for v in q]

    positions = jnp.arange(512, dtype=jnp.int32)
    ends = jnp.sum(
        jnp.where(jnp.arange(8)[:, None] <= jnp.arange(8)[None, :], lengths[:, None], 0), axis=0
    )
    request = jnp.sum((positions[:, None] >= ends[None, :]).astype(jnp.int32), axis=1)
    adapter_hot = request_adapter[:, None] == jnp.arange(128, dtype=jnp.int32)[None, :]
    slots = jnp.sum(jnp.where(adapter_hot, placement[None, :], 0), axis=1)

    slot_r = jnp.sum(jnp.where(jnp.arange(8) == ten, slots, 0))
    rows_b = lax.dynamic_slice_in_dim(b_down, (slot_r & 7) * R, R, axis=0)
    rows_b = jnp.where(slot_r >> 3 == adp, rows_b, jnp.zeros_like(rows_b))
    rows_b = rows_b.reshape(R, 4, 4, 512).transpose(2, 1, 0, 3)
    got = [block(rows_b, me["z"])]
    got += [shift(block(rows_b, (me["z"] + s) & 3), "z", s) for s in (1, 2, 3)]
    rows_b = sum(v.astype(F32) for v in got).astype(BF)
    blk = jnp.arange(8, dtype=jnp.int32)
    blk_request = ((me["y"] - blk) & 3) << 1 | (me["c"] + (blk >> 2)) & 1

    wide = jnp.arange(2048, dtype=jnp.int32)
    rank = jnp.arange(128, dtype=jnp.int32)
    own_adapter = jnp.sum(
        jnp.where((rank >> 4)[:, None] == jnp.arange(8)[None, :], request_adapter[None, :], 0), axis=1
    )
    pick = (wide[:, None] == ((own_adapter << 4) | (rank & 15))[None, :]).astype(BF)
    take = (((0,), (0,)), ((), ()))
    gate_rows = lax.dot_general(pick, b_gate, take, preferred_element_type=F32).astype(BF)
    up_rows = lax.dot_general(pick, b_up, take, preferred_element_type=F32).astype(BF)
    down_cols = jnp.dot(a_down, pick, preferred_element_type=F32).astype(BF)

    unit = jnp.concatenate(
        [jnp.zeros((224, 128), BF), jnp.eye(R, 128, dtype=BF), jnp.zeros((16, 128), BF)], axis=0
    )
    w_blocks = w_down.reshape(16, 224, 512)

    tok = jnp.arange(512, dtype=jnp.int32)
    held = row_order(me, ("z", "x", "y"))
    get = (held[:, None] == tok[None, :]).astype(BF)
    row_request = jnp.sum((held[:, None] >= ends[None, :]).astype(jnp.int32), axis=1)
    row_slot = jnp.sum(
        jnp.where(row_request[:, None] == jnp.arange(8)[None, :], slots[None, :], 0), axis=1
    )
    own_slot = jnp.where(row_slot >> 3 == adp, row_slot & 7, -1)

    gate, up, picked = products(
        p, q, w_gate, w_up, a_gate, a_up, own_slot[:, None], get
    )

    picked = sum(v.astype(F32) for v in gather4(picked, "z")).astype(BF)
    sent = [
        jnp.concatenate([picked, block(rows_b, (me["x"] + s) & 3)], axis=0) for s in range(4)
    ]
    got = [sent[0]] + [shift(sent[s], "x", s) for s in (1, 2, 3)]
    both = sum(v.astype(F32) for v in got).astype(BF)
    picked, rows_b = both[: 2 * R], both[2 * R :]
    hidden = hidden_of(gate, up, picked, get, row_request[:, None], gate_rows, up_rows, down_cols)

    def spread_block(low, hot):
        return jnp.where(hot[:, :, None], low[:, None, :], jnp.zeros_like(low)[:, None, :]).reshape(
            low.shape[0], -1
        )

    ways = (("x", "z"), ("z", "x"))
    first = [
        jnp.stack(gather4(hidden[i * 256 : i * 256 + 256], way[0]), axis=0)
        for i, way in enumerate(ways)
    ]
    *first, rows_b = lax.optimization_barrier((*first, rows_b))
    pieces = [ring4(h, way[1]) for h, way in zip(first, ways)]
    rows_b = jnp.concatenate(gather4(rows_b, "y"), axis=0)
    rows_b = jnp.concatenate([rows_b, shift(rows_b, "c", 1)], axis=0)
    base = []
    for (own, near, low_half, high_half, far), way in zip(pieces, ways):
        acc = 0.0
        for r2, piece in ((0, own), (1, near), (3, far), (2, low_half), (2, high_half)):
            for i in range(piece.shape[0]):
                r1 = i + 2 if piece is high_half else i
                at = {way[0]: (me[way[0]] - r1) & 3, way[1]: (me[way[1]] - r2) & 3}
                w = block(w_blocks, at["x"] << 2 | at["z"])
                w = jnp.concatenate([w, jnp.zeros((32, 512), BF)], axis=0)
                w = jnp.concatenate([w, unit], axis=1)
                acc = acc + jnp.dot(piece[i], w, preferred_element_type=F32)
        base.append(acc)
    base = jnp.concatenate(base, axis=0)
    hot_blk = request[:, None] == blk_request[None, :]
    delta = jnp.dot(
        spread_block(base[:, 512 : 512 + R].astype(BF), hot_blk), rows_b, preferred_element_type=F32
    )
    out = (base[:, :512] + delta).reshape(4, 2, 64, 512)

    got = shift(jnp.where(me["c"] == 0, out[:, 1], out[:, 0]).astype(BF), "c", 1)
    out = jnp.where(me["c"] == 0, out[:, 0], out[:, 1]) + got.astype(F32)
    out = out.astype(BF).reshape(64, 4, 512)
    same = [[(2 * y + c) * 16 + a for y in range(4) for a in range(16)] for c in range(2)]
    got = lax.all_to_all(
        out, ("tensor", "adapter"), 0, 0, tiled=True, axis_index_groups=same
    )
    mixed = jnp.sum(got.reshape(4, 16, 4, 512).astype(F32), axis=0).astype(BF)
    return mixed.transpose(1, 0, 2).reshape(4, D)


def solution(mesh):
    in_specs = (
        P(("tensor", "adapter"), None),
        P(None, ("tensor", "adapter")),
        P(None, ("tensor", "adapter")),
        P("tensor", "adapter"),
        P(None, "adapter"),
        P(None, "adapter"),
        P(None, ("tensor", "adapter")),
        P(None, ("tensor", "adapter")),
        P(("tensor", "adapter"), None),
        P("adapter", None),
        P(),
        P(),
        P(),
    )
    out_specs = P(("tensor", "adapter"), None)
    return jax.shard_map(local, mesh=mesh, in_specs=in_specs, out_specs=out_specs, check_vma=False)
```

```python
import jax
import jax.numpy as jnp
from jax import lax
from jax.experimental import pallas as pl
from jax.experimental.pallas import tpu as pltpu
from jax.sharding import PartitionSpec as P

R = 16
N4 = 4

BF = jnp.bfloat16
F32 = jnp.float32


def shift(v, axis, s):
    if axis == "c":
        return lax.ppermute(v, "tensor", [(t, t ^ 1) for t in range(8)])
    if axis == "y":
        return lax.ppermute(v, "tensor", [(t, (t + 2 * s) % 8) for t in range(8)])
    if axis == "x":
        return lax.ppermute(v, "adapter", [(a, (a + 4 * s) % 16) for a in range(16)])
    return lax.ppermute(v, "adapter", [(a, a - a % 4 + (a + s) % 4) for a in range(16)])


def gather4(v, axis):
    return [v] + [shift(v, axis, s) for s in (1, 2, 3)]


def ring4(v, axis):
    n = v.shape[0] // 2
    near, far = shift(v, axis, 1), shift(v, axis, 3)
    return [v, near, shift(near[:n], axis, 1), shift(far[n:], axis, 3), far]


def coords():
    t, a = lax.axis_index("tensor"), lax.axis_index("adapter")
    return {"y": t >> 1, "c": t & 1, "x": a >> 2, "z": a & 3}


KB = 1024


def products_kernel(*refs):
    p, q = refs[:8], refs[8:16]
    wg, wu, ag, au, own_slot, get, gate, up, picked, shrunk = refs[16:]
    k = pl.program_id(0)
    steps = pl.num_programs(0) // 2

    @pl.when(k == 0)
    def _():
        gate[...] = jnp.zeros_like(gate)
        up[...] = jnp.zeros_like(up)
        shrunk[...] = jnp.zeros_like(shrunk)

    def add(rows):
        last = (((1,), (1,)), ((), ()))
        gate[...] += lax.dot_general(rows, wg[...], last, preferred_element_type=F32)
        up[...] += lax.dot_general(rows, wu[...], last, preferred_element_type=F32)
        a = jnp.concatenate([ag[...], au[...]], axis=1)
        shrunk[...] += jnp.dot(rows, a, preferred_element_type=F32)

    @pl.when(k < steps)
    def _():
        add(jnp.concatenate([v[...] for v in p], axis=0))

    @pl.when(k >= steps)
    def _():
        add(
            jnp.concatenate(
                [
                    q[c * 4 + x][y * 16 : y * 16 + 16, :]
                    for c in range(2)
                    for y in range(4)
                    for x in range(4)
                ],
                axis=0,
            )
        )

    @pl.when(k == pl.num_programs(0) - 1)
    def _():
        lane = lax.broadcasted_iota(jnp.int32, (512, 256), 1)
        kept = jnp.where(own_slot[...] == (lane & 127) >> 4, shrunk[...], 0.0).astype(BF)
        fold = one_hot((256, 128), lambda r, c: (r & 15 | (r >> 7) << 4) == c)
        kept = jnp.dot(kept, fold, preferred_element_type=F32)
        kept = kept.T.astype(BF)[:32]
        picked[...] = jnp.dot(kept, get[...], preferred_element_type=F32).astype(BF)


def one_hot(shape, test):
    r = lax.broadcasted_iota(jnp.int32, shape, 0)
    c = lax.broadcasted_iota(jnp.int32, shape, 1)
    return jnp.where(test(r, c), 1.0, 0.0).astype(BF)


def hidden_kernel(gate, up, shrunk, get, row_request, gate_rows, up_rows, down_cols, out):
    last = (((1,), (1,)), ((), ()))
    low = lax.dot_general(get[...], shrunk[...], last, preferred_element_type=F32).astype(BF)
    wide = one_hot((2 * R, 256), lambda r, c: (c & 15 | (c >> 7) << 4) == r)
    low = jnp.dot(low, wide, preferred_element_type=F32)
    lane = lax.broadcasted_iota(jnp.int32, (512, 256), 1)
    hot = row_request[...] == (lane & 127) >> 4
    low = jnp.where(hot, low, 0.0).astype(BF)
    g = gate[...] + lax.dot_general(low[:, :128], gate_rows[...], last, preferred_element_type=F32)
    u = up[...] + lax.dot_general(low[:, 128:], up_rows[...], last, preferred_element_type=F32)
    hidden = (g / (1.0 + jnp.exp(-g)) * u).astype(BF)
    down = jnp.dot(hidden, down_cols[...], preferred_element_type=F32)
    down = jnp.where(hot[:, :128], down, 0.0).astype(BF)
    units = hidden.shape[1]
    place = one_hot((units, 256), lambda r, c: r == c)
    after = one_hot((128, 256), lambda r, c: (r & 15) + units == c)
    both = jnp.dot(hidden, place, preferred_element_type=F32)
    both = (both + jnp.dot(down, after, preferred_element_type=F32)).astype(BF)
    first = (((0,), (0,)), ((), ()))
    out[...] = lax.dot_general(get[...], both, first, preferred_element_type=F32).astype(BF)


def hidden_of(*args):
    return pl.pallas_call(
        hidden_kernel,
        out_shape=jax.ShapeDtypeStruct((512, 256), BF),
        compiler_params=pltpu.CompilerParams(vmem_limit_bytes=12 << 20),
        name="hidden",
    )(*args)


def products(p, q, w_gate, w_up, a_gate, a_up, own_slot, get):
    half = p[0].shape[1]
    steps = half // KB
    rows = [pl.BlockSpec((v.shape[0], KB), lambda k: (0, jnp.minimum(k, steps - 1))) for v in p]
    rows += [pl.BlockSpec((v.shape[0], KB), lambda k: (0, jnp.maximum(k - steps, 0))) for v in q]
    units = w_gate.shape[1]
    cols = [pl.BlockSpec((units, KB), lambda k: (0, k))] * 2
    cols += [pl.BlockSpec((KB, 128), lambda k: (k, 0))] * 2
    cols += [pl.BlockSpec((512, 1), lambda k: (0, 0)), pl.BlockSpec((512, 512), lambda k: (0, 0))]
    return pl.pallas_call(
        products_kernel,
        grid=(2 * steps,),
        in_specs=rows + cols,
        out_specs=[
            pl.BlockSpec((512, units), lambda k: (0, 0)),
            pl.BlockSpec((512, units), lambda k: (0, 0)),
            pl.BlockSpec((2 * R, 512), lambda k: (0, 0)),
        ],
        out_shape=[
            pltpu.HBM((512, units), F32),
            pltpu.HBM((512, units), F32),
            jax.ShapeDtypeStruct((2 * R, 512), BF),
        ],
        scratch_shapes=[pltpu.VMEM((512, 256), F32)],
        compiler_params=pltpu.CompilerParams(vmem_limit_bytes=20 << 20),
        name="products",
    )(*p, *q, w_gate.T, w_up.T, a_gate, a_up, own_slot, get)


def row_order(me, order):
    row = jnp.arange(512, dtype=jnp.int32)
    at = {}
    at[order[0]] = (me[order[0]] - (row >> 2)) & 3
    at[order[1]] = (me[order[1]] - (row >> 4)) & 3
    at[order[2]] = (me[order[2]] - (row >> 6)) & 3
    at["c"] = (me["c"] + (row >> 8)) & 1
    return (at["y"] << 7) | (at["c"] << 6) | (at["x"] << 4) | (at["z"] << 2) | (row & 3)


def block(v, at):
    return lax.dynamic_index_in_dim(v, at, 0, keepdims=False)


def local(
    tokens_in,
    w_gate,
    w_up,
    w_down,
    a_gate,
    a_up,
    b_gate,
    b_up,
    a_down,
    b_down,
    lengths,
    request_adapter,
    placement,
):
    me = coords()
    D = tokens_in.shape[1]

    half = D // 2
    v = jnp.concatenate(gather4(tokens_in, "z"), axis=0)
    p = jnp.concatenate(gather4(v[:, :half], "x"), axis=0)
    q = jnp.concatenate(gather4(v[:, half:], "y"), axis=0)
    p, q, lengths, request_adapter, placement, ten, adp = lax.optimization_barrier(
        (p, q, lengths, request_adapter, placement, lax.axis_index("tensor"), lax.axis_index("adapter"))
    )
    me = {"y": ten >> 1, "c": ten & 1, "x": adp >> 2, "z": adp & 3}
    p, q = gather4(p, "y"), gather4(q, "x")
    p = p + [shift(v, "c", 1) for v in p]
    q = q + [shift(v, "c", 1) for v in q]

    positions = jnp.arange(512, dtype=jnp.int32)
    ends = jnp.sum(
        jnp.where(jnp.arange(8)[:, None] <= jnp.arange(8)[None, :], lengths[:, None], 0), axis=0
    )
    request = jnp.sum((positions[:, None] >= ends[None, :]).astype(jnp.int32), axis=1)
    adapter_hot = request_adapter[:, None] == jnp.arange(128, dtype=jnp.int32)[None, :]
    slots = jnp.sum(jnp.where(adapter_hot, placement[None, :], 0), axis=1)

    slot_r = jnp.sum(jnp.where(jnp.arange(8) == ten, slots, 0))
    rows_b = lax.dynamic_slice_in_dim(b_down, (slot_r & 7) * R, R, axis=0)
    rows_b = jnp.where(slot_r >> 3 == adp, rows_b, jnp.zeros_like(rows_b))
    rows_b = rows_b.reshape(R, 4, 4, 512).transpose(2, 1, 0, 3)
    got = [block(rows_b, me["z"])]
    got += [shift(block(rows_b, (me["z"] + s) & 3), "z", s) for s in (1, 2, 3)]
    rows_b = sum(v.astype(F32) for v in got).astype(BF)
    blk = jnp.arange(8, dtype=jnp.int32)
    blk_request = ((me["y"] - blk) & 3) << 1 | (me["c"] + (blk >> 2)) & 1

    wide = jnp.arange(2048, dtype=jnp.int32)
    rank = jnp.arange(128, dtype=jnp.int32)
    own_adapter = jnp.sum(
        jnp.where((rank >> 4)[:, None] == jnp.arange(8)[None, :], request_adapter[None, :], 0), axis=1
    )
    pick = (wide[:, None] == ((own_adapter << 4) | (rank & 15))[None, :]).astype(BF)
    take = (((0,), (0,)), ((), ()))
    gate_rows = lax.dot_general(b_gate, pick, take, preferred_element_type=F32).astype(BF)
    up_rows = lax.dot_general(b_up, pick, take, preferred_element_type=F32).astype(BF)
    down_cols = jnp.dot(a_down, pick, preferred_element_type=F32).astype(BF)

    unit = jnp.concatenate(
        [jnp.zeros((224, 128), BF), jnp.eye(R, 128, dtype=BF), jnp.zeros((16, 128), BF)], axis=0
    )
    w_blocks = w_down.reshape(16, 224, 512)

    tok = jnp.arange(512, dtype=jnp.int32)
    held = row_order(me, ("z", "x", "y"))
    get = (held[:, None] == tok[None, :]).astype(BF)
    row_request = jnp.sum((held[:, None] >= ends[None, :]).astype(jnp.int32), axis=1)
    row_slot = jnp.sum(
        jnp.where(row_request[:, None] == jnp.arange(8)[None, :], slots[None, :], 0), axis=1
    )
    own_slot = jnp.where(row_slot >> 3 == adp, row_slot & 7, -1)

    gate, up, picked = products(
        p, q, w_gate, w_up, a_gate, a_up, own_slot[:, None], get
    )

    picked = sum(v.astype(F32) for v in gather4(picked, "z")).astype(BF)
    sent = [
        jnp.concatenate([picked, block(rows_b, (me["x"] + s) & 3)], axis=0) for s in range(4)
    ]
    got = [sent[0]] + [shift(sent[s], "x", s) for s in (1, 2, 3)]
    both = sum(v.astype(F32) for v in got).astype(BF)
    picked, rows_b = both[: 2 * R], both[2 * R :]
    hidden = hidden_of(gate, up, picked, get, row_request[:, None], gate_rows, up_rows, down_cols)

    def spread_block(low, hot):
        return jnp.where(hot[:, :, None], low[:, None, :], jnp.zeros_like(low)[:, None, :]).reshape(
            low.shape[0], -1
        )

    ways = (("x", "z"), ("z", "x"))
    first = [gather4(hidden[i * 256 : i * 256 + 256], way[0]) for i, way in enumerate(ways)]
    first[0][1], rows_b = lax.optimization_barrier((first[0][1], rows_b))
    rows_b = jnp.concatenate(gather4(rows_b, "y"), axis=0)
    first = lax.optimization_barrier([jnp.stack(v, axis=0) for v in first])
    pieces = [ring4(h, way[1]) for h, way in zip(first, ways)]
    rows_b = jnp.concatenate([rows_b, shift(rows_b, "c", 1)], axis=0)
    base = []
    for (own, near, low_half, high_half, far), way in zip(pieces, ways):
        acc = 0.0
        for r2, piece in ((0, own), (1, near), (3, far), (2, low_half), (2, high_half)):
            for i in range(piece.shape[0]):
                r1 = i + 2 if piece is high_half else i
                at = {way[0]: (me[way[0]] - r1) & 3, way[1]: (me[way[1]] - r2) & 3}
                w = block(w_blocks, at["x"] << 2 | at["z"])
                w = jnp.concatenate([w, jnp.zeros((32, 512), BF)], axis=0)
                w = jnp.concatenate([w, unit], axis=1)
                acc = acc + jnp.dot(piece[i], w, preferred_element_type=F32)
        base.append(acc)
    base = jnp.concatenate(base, axis=0)
    hot_blk = request[:, None] == blk_request[None, :]
    delta = jnp.dot(
        spread_block(base[:, 512 : 512 + R].astype(BF), hot_blk), rows_b, preferred_element_type=F32
    )
    out = (base[:, :512] + delta).reshape(4, 2, 64, 512)

    got = shift(jnp.where(me["c"] == 0, out[:, 1], out[:, 0]).astype(BF), "c", 1)
    out = jnp.where(me["c"] == 0, out[:, 0], out[:, 1]) + got.astype(F32)
    out = out.astype(BF).reshape(64, 4, 512)
    same = [[(2 * y + c) * 16 + a for y in range(4) for a in range(16)] for c in range(2)]
    got = lax.all_to_all(
        out, ("tensor", "adapter"), 0, 0, tiled=True, axis_index_groups=same
    )
    mixed = jnp.sum(got.reshape(4, 16, 4, 512).astype(F32), axis=0).astype(BF)
    return mixed.transpose(1, 0, 2).reshape(4, D)


def solution(mesh):
    in_specs = (
        P(("tensor", "adapter"), None),
        P(None, ("tensor", "adapter")),
        P(None, ("tensor", "adapter")),
        P("tensor", "adapter"),
        P(None, "adapter"),
        P(None, "adapter"),
        P(None, ("tensor", "adapter")),
        P(None, ("tensor", "adapter")),
        P(("tensor", "adapter"), None),
        P("adapter", None),
        P(),
        P(),
        P(),
    )
    out_specs = P(("tensor", "adapter"), None)
    return jax.shard_map(local, mesh=mesh, in_specs=in_specs, out_specs=out_specs, check_vma=False)
```

```python
import jax
import jax.numpy as jnp
from jax import lax
from jax.experimental import pallas as pl
from jax.experimental.pallas import tpu as pltpu
from jax.sharding import PartitionSpec as P

R = 16
N4 = 4

BF = jnp.bfloat16
F32 = jnp.float32


def shift(v, axis, s):
    if axis == "c":
        return lax.ppermute(v, "tensor", [(t, t ^ 1) for t in range(8)])
    if axis == "y":
        return lax.ppermute(v, "tensor", [(t, (t + 2 * s) % 8) for t in range(8)])
    if axis == "x":
        return lax.ppermute(v, "adapter", [(a, (a + 4 * s) % 16) for a in range(16)])
    return lax.ppermute(v, "adapter", [(a, a - a % 4 + (a + s) % 4) for a in range(16)])


def gather4(v, axis):
    return [v] + [shift(v, axis, s) for s in (1, 2, 3)]


def ring4(v, axis):
    n = v.shape[0] // 2
    near, far = shift(v, axis, 1), shift(v, axis, 3)
    return [v, near, shift(near[:n], axis, 1), shift(far[n:], axis, 3), far]


def coords():
    t, a = lax.axis_index("tensor"), lax.axis_index("adapter")
    return {"y": t >> 1, "c": t & 1, "x": a >> 2, "z": a & 3}


KB = 1024


def products_kernel(*refs):
    p, q = refs[:8], refs[8:16]
    wg, wu, ag, au, own_slot, get, gate, up, picked, shrunk = refs[16:]
    k = pl.program_id(0)
    steps = pl.num_programs(0) // 2

    @pl.when(k == 0)
    def _():
        gate[...] = jnp.zeros_like(gate)
        up[...] = jnp.zeros_like(up)
        shrunk[...] = jnp.zeros_like(shrunk)

    def add(rows):
        last = (((1,), (1,)), ((), ()))
        gate[...] += lax.dot_general(rows, wg[...], last, preferred_element_type=F32)
        up[...] += lax.dot_general(rows, wu[...], last, preferred_element_type=F32)
        a = jnp.concatenate([ag[...], au[...]], axis=1)
        shrunk[...] += jnp.dot(rows, a, preferred_element_type=F32)

    @pl.when(k < steps)
    def _():
        add(jnp.concatenate([v[...] for v in p], axis=0))

    @pl.when(k >= steps)
    def _():
        add(
            jnp.concatenate(
                [
                    q[c * 4 + x][y * 16 : y * 16 + 16, :]
                    for c in range(2)
                    for y in range(4)
                    for x in range(4)
                ],
                axis=0,
            )
        )

    @pl.when(k == pl.num_programs(0) - 1)
    def _():
        lane = lax.broadcasted_iota(jnp.int32, (512, 256), 1)
        kept = jnp.where(own_slot[...] == (lane & 127) >> 4, shrunk[...], 0.0).astype(BF)
        fold = one_hot((256, 128), lambda r, c: (r & 15 | (r >> 7) << 4) == c)
        kept = jnp.dot(kept, fold, preferred_element_type=F32)
        kept = kept.T.astype(BF)[:32]
        picked[...] = jnp.dot(kept, get[...], preferred_element_type=F32).astype(BF)


def in_hbm(v):
    return pltpu.with_memory_space_constraint(v, pltpu.HBM)


def one_hot(shape, test):
    r = lax.broadcasted_iota(jnp.int32, shape, 0)
    c = lax.broadcasted_iota(jnp.int32, shape, 1)
    return jnp.where(test(r, c), 1.0, 0.0).astype(BF)


def hidden_kernel(gate, up, shrunk, get, row_request, gate_rows, up_rows, down_cols, out):
    last = (((1,), (1,)), ((), ()))
    low = lax.dot_general(get[...], shrunk[...], last, preferred_element_type=F32).astype(BF)
    wide = one_hot((2 * R, 256), lambda r, c: (c & 15 | (c >> 7) << 4) == r)
    low = jnp.dot(low, wide, preferred_element_type=F32)
    lane = lax.broadcasted_iota(jnp.int32, (512, 256), 1)
    hot = row_request[...] == (lane & 127) >> 4
    low = jnp.where(hot, low, 0.0).astype(BF)
    g = gate[...] + lax.dot_general(low[:, :128], gate_rows[...], last, preferred_element_type=F32)
    u = up[...] + lax.dot_general(low[:, 128:], up_rows[...], last, preferred_element_type=F32)
    hidden = (g / (1.0 + jnp.exp(-g)) * u).astype(BF)
    down = jnp.dot(hidden, down_cols[...], preferred_element_type=F32)
    down = jnp.where(hot[:, :128], down, 0.0).astype(BF)
    units = hidden.shape[1]
    place = one_hot((units, 256), lambda r, c: r == c)
    after = one_hot((128, 256), lambda r, c: (r & 15) + units == c)
    both = jnp.dot(hidden, place, preferred_element_type=F32)
    both = (both + jnp.dot(down, after, preferred_element_type=F32)).astype(BF)
    first = (((0,), (0,)), ((), ()))
    out[...] = lax.dot_general(get[...], both, first, preferred_element_type=F32).astype(BF)


def hidden_of(*args):
    return pl.pallas_call(
        hidden_kernel,
        out_shape=jax.ShapeDtypeStruct((512, 256), BF),
        compiler_params=pltpu.CompilerParams(vmem_limit_bytes=12 << 20),
        name="hidden",
    )(*args)


def products(p, q, w_gate, w_up, a_gate, a_up, own_slot, get):
    half = p[0].shape[1]
    steps = half // KB
    rows = [pl.BlockSpec((v.shape[0], KB), lambda k: (0, jnp.minimum(k, steps - 1))) for v in p]
    rows += [pl.BlockSpec((v.shape[0], KB), lambda k: (0, jnp.maximum(k - steps, 0))) for v in q]
    units = w_gate.shape[1]
    cols = [pl.BlockSpec((units, KB), lambda k: (0, k))] * 2
    cols += [pl.BlockSpec((KB, 128), lambda k: (k, 0))] * 2
    cols += [pl.BlockSpec((512, 1), lambda k: (0, 0)), pl.BlockSpec((512, 512), lambda k: (0, 0))]
    return pl.pallas_call(
        products_kernel,
        grid=(2 * steps,),
        in_specs=rows + cols,
        out_specs=[
            pl.BlockSpec((512, units), lambda k: (0, 0)),
            pl.BlockSpec((512, units), lambda k: (0, 0)),
            pl.BlockSpec((2 * R, 512), lambda k: (0, 0)),
        ],
        out_shape=[
            pltpu.HBM((512, units), F32),
            pltpu.HBM((512, units), F32),
            jax.ShapeDtypeStruct((2 * R, 512), BF),
        ],
        scratch_shapes=[pltpu.VMEM((512, 256), F32)],
        compiler_params=pltpu.CompilerParams(vmem_limit_bytes=20 << 20),
        name="products",
    )(*p, *q, in_hbm(w_gate.T), in_hbm(w_up.T), in_hbm(a_gate), in_hbm(a_up), own_slot, get)


def row_order(me, order):
    row = jnp.arange(512, dtype=jnp.int32)
    at = {}
    at[order[0]] = (me[order[0]] - (row >> 2)) & 3
    at[order[1]] = (me[order[1]] - (row >> 4)) & 3
    at[order[2]] = (me[order[2]] - (row >> 6)) & 3
    at["c"] = (me["c"] + (row >> 8)) & 1
    return (at["y"] << 7) | (at["c"] << 6) | (at["x"] << 4) | (at["z"] << 2) | (row & 3)


def block(v, at):
    return lax.dynamic_index_in_dim(v, at, 0, keepdims=False)


def local(
    tokens_in,
    w_gate,
    w_up,
    w_down,
    a_gate,
    a_up,
    b_gate,
    b_up,
    a_down,
    b_down,
    lengths,
    request_adapter,
    placement,
):
    me = coords()
    D = tokens_in.shape[1]

    half = D // 2
    v = jnp.concatenate(gather4(tokens_in, "z"), axis=0)
    p = jnp.concatenate(gather4(v[:, :half], "x"), axis=0)
    q = jnp.concatenate(gather4(v[:, half:], "y"), axis=0)
    p, q, lengths, request_adapter, placement, ten, adp = lax.optimization_barrier(
        (p, q, lengths, request_adapter, placement, lax.axis_index("tensor"), lax.axis_index("adapter"))
    )
    me = {"y": ten >> 1, "c": ten & 1, "x": adp >> 2, "z": adp & 3}
    p, q = gather4(p, "y"), gather4(q, "x")
    p = p + [shift(v, "c", 1) for v in p]
    q = q + [shift(v, "c", 1) for v in q]

    positions = jnp.arange(512, dtype=jnp.int32)
    ends = jnp.sum(
        jnp.where(jnp.arange(8)[:, None] <= jnp.arange(8)[None, :], lengths[:, None], 0), axis=0
    )
    request = jnp.sum((positions[:, None] >= ends[None, :]).astype(jnp.int32), axis=1)
    adapter_hot = request_adapter[:, None] == jnp.arange(128, dtype=jnp.int32)[None, :]
    slots = jnp.sum(jnp.where(adapter_hot, placement[None, :], 0), axis=1)

    slot_r = jnp.sum(jnp.where(jnp.arange(8) == ten, slots, 0))
    rows_b = lax.dynamic_slice_in_dim(b_down, (slot_r & 7) * R, R, axis=0)
    rows_b = jnp.where(slot_r >> 3 == adp, rows_b, jnp.zeros_like(rows_b))
    rows_b = rows_b.reshape(R, 4, 4, 512).transpose(2, 1, 0, 3)
    got = [block(rows_b, me["z"])]
    got += [shift(block(rows_b, (me["z"] + s) & 3), "z", s) for s in (1, 2, 3)]
    rows_b = sum(v.astype(F32) for v in got).astype(BF)
    blk = jnp.arange(8, dtype=jnp.int32)
    blk_request = ((me["y"] - blk) & 3) << 1 | (me["c"] + (blk >> 2)) & 1

    unit = jnp.concatenate(
        [jnp.zeros((224, 128), BF), jnp.eye(R, 128, dtype=BF), jnp.zeros((16, 128), BF)], axis=0
    )
    w_blocks = w_down.reshape(16, 224, 512)

    tok = jnp.arange(512, dtype=jnp.int32)
    held = row_order(me, ("z", "x", "y"))
    get = (held[:, None] == tok[None, :]).astype(BF)
    row_request = jnp.sum((held[:, None] >= ends[None, :]).astype(jnp.int32), axis=1)
    row_slot = jnp.sum(
        jnp.where(row_request[:, None] == jnp.arange(8)[None, :], slots[None, :], 0), axis=1
    )
    own_slot = jnp.where(row_slot >> 3 == adp, row_slot & 7, -1)

    gate, up, picked = products(
        p, q, w_gate, w_up, a_gate, a_up, own_slot[:, None], get
    )

    picked, request_adapter = lax.optimization_barrier((picked, request_adapter))
    wide = jnp.arange(2048, dtype=jnp.int32)
    rank = jnp.arange(128, dtype=jnp.int32)
    own_adapter = jnp.sum(
        jnp.where((rank >> 4)[:, None] == jnp.arange(8)[None, :], request_adapter[None, :], 0), axis=1
    )
    pick = (wide[:, None] == ((own_adapter << 4) | (rank & 15))[None, :]).astype(BF)
    take = (((0,), (0,)), ((), ()))
    gate_rows = lax.dot_general(b_gate, pick, take, preferred_element_type=F32).astype(BF)
    up_rows = lax.dot_general(b_up, pick, take, preferred_element_type=F32).astype(BF)
    down_cols = jnp.dot(a_down, pick, preferred_element_type=F32).astype(BF)

    picked = sum(v.astype(F32) for v in gather4(picked, "z")).astype(BF)
    sent = [
        jnp.concatenate([picked, block(rows_b, (me["x"] + s) & 3)], axis=0) for s in range(4)
    ]
    got = [sent[0]] + [shift(sent[s], "x", s) for s in (1, 2, 3)]
    both = sum(v.astype(F32) for v in got).astype(BF)
    picked, rows_b = both[: 2 * R], both[2 * R :]
    hidden = hidden_of(in_hbm(gate), in_hbm(up), picked, get, row_request[:, None], gate_rows, up_rows, down_cols)

    def spread_block(low, hot):
        return jnp.where(hot[:, :, None], low[:, None, :], jnp.zeros_like(low)[:, None, :]).reshape(
            low.shape[0], -1
        )

    ways = (("x", "z"), ("z", "x"))
    first = [gather4(hidden[i * 256 : i * 256 + 256], way[0]) for i, way in enumerate(ways)]
    first[0][1], rows_b = lax.optimization_barrier((first[0][1], rows_b))
    rows_b = jnp.concatenate(gather4(rows_b, "y"), axis=0)
    first = lax.optimization_barrier([jnp.stack(v, axis=0) for v in first])
    pieces = [ring4(h, way[1]) for h, way in zip(first, ways)]
    rows_b = jnp.concatenate([rows_b, shift(rows_b, "c", 1)], axis=0)
    base = []
    for (own, near, low_half, high_half, far), way in zip(pieces, ways):
        acc = 0.0
        for r2, piece in ((0, own), (1, near), (3, far), (2, low_half), (2, high_half)):
            for i in range(piece.shape[0]):
                r1 = i + 2 if piece is high_half else i
                at = {way[0]: (me[way[0]] - r1) & 3, way[1]: (me[way[1]] - r2) & 3}
                w = block(w_blocks, at["x"] << 2 | at["z"])
                w = jnp.concatenate([w, jnp.zeros((32, 512), BF)], axis=0)
                w = jnp.concatenate([w, unit], axis=1)
                acc = acc + jnp.dot(piece[i], w, preferred_element_type=F32)
        base.append(acc)
    base = jnp.concatenate(base, axis=0)
    hot_blk = request[:, None] == blk_request[None, :]
    delta = jnp.dot(
        spread_block(base[:, 512 : 512 + R].astype(BF), hot_blk), rows_b, preferred_element_type=F32
    )
    out = (base[:, :512] + delta).reshape(4, 2, 64, 512)

    got = shift(jnp.where(me["c"] == 0, out[:, 1], out[:, 0]).astype(BF), "c", 1)
    out = jnp.where(me["c"] == 0, out[:, 0], out[:, 1]) + got.astype(F32)
    out = out.astype(BF).reshape(64, 4, 512)
    same = [[(2 * y + c) * 16 + a for y in range(4) for a in range(16)] for c in range(2)]
    got = lax.all_to_all(
        out, ("tensor", "adapter"), 0, 0, tiled=True, axis_index_groups=same
    )
    mixed = jnp.sum(got.reshape(4, 16, 4, 512).astype(F32), axis=0).astype(BF)
    return mixed.transpose(1, 0, 2).reshape(4, D)


def solution(mesh):
    in_specs = (
        P(("tensor", "adapter"), None),
        P(None, ("tensor", "adapter")),
        P(None, ("tensor", "adapter")),
        P("tensor", "adapter"),
        P(None, "adapter"),
        P(None, "adapter"),
        P(None, ("tensor", "adapter")),
        P(None, ("tensor", "adapter")),
        P(("tensor", "adapter"), None),
        P("adapter", None),
        P(),
        P(),
        P(),
    )
    out_specs = P(("tensor", "adapter"), None)
    return jax.shard_map(local, mesh=mesh, in_specs=in_specs, out_specs=out_specs, check_vma=False)
```

```python
import jax
import jax.numpy as jnp
from jax import lax
from jax.experimental import pallas as pl
from jax.experimental.pallas import tpu as pltpu
from jax.sharding import PartitionSpec as P

R = 16
N4 = 4

BF = jnp.bfloat16
F32 = jnp.float32


def shift(v, axis, s):
    if axis == "c":
        return lax.ppermute(v, "tensor", [(t, t ^ 1) for t in range(8)])
    if axis == "y":
        return lax.ppermute(v, "tensor", [(t, (t + 2 * s) % 8) for t in range(8)])
    if axis == "x":
        return lax.ppermute(v, "adapter", [(a, (a + 4 * s) % 16) for a in range(16)])
    return lax.ppermute(v, "adapter", [(a, a - a % 4 + (a + s) % 4) for a in range(16)])


def gather4(v, axis):
    return [v] + [shift(v, axis, s) for s in (1, 2, 3)]


def ring4(v, axis):
    n = v.shape[0] // 2
    near, far = shift(v, axis, 1), shift(v, axis, 3)
    return [v, near, shift(near[:n], axis, 1), shift(far[n:], axis, 3), far]


def coords():
    t, a = lax.axis_index("tensor"), lax.axis_index("adapter")
    return {"y": t >> 1, "c": t & 1, "x": a >> 2, "z": a & 3}


KB = 2048


def products_kernel(*refs):
    p, q = refs[:8], refs[8:16]
    wg, wu, ag, au, own_slot, get, gate, up, picked, shrunk = refs[16:]
    k = pl.program_id(0)
    steps = pl.num_programs(0) // 2

    @pl.when(k == 0)
    def _():
        gate[...] = jnp.zeros_like(gate)
        up[...] = jnp.zeros_like(up)
        shrunk[...] = jnp.zeros_like(shrunk)

    def add(rows):
        last = (((1,), (1,)), ((), ()))
        gate[...] += lax.dot_general(rows, wg[...], last, preferred_element_type=F32)
        up[...] += lax.dot_general(rows, wu[...], last, preferred_element_type=F32)
        a = jnp.concatenate([ag[...], au[...]], axis=1)
        shrunk[...] += jnp.dot(rows, a, preferred_element_type=F32)

    @pl.when(k < steps)
    def _():
        add(jnp.concatenate([v[...] for v in p], axis=0))

    @pl.when(k >= steps)
    def _():
        add(
            jnp.concatenate(
                [
                    q[c * 4 + x][y * 16 : y * 16 + 16, :]
                    for c in range(2)
                    for y in range(4)
                    for x in range(4)
                ],
                axis=0,
            )
        )

    @pl.when(k == pl.num_programs(0) - 1)
    def _():
        lane = lax.broadcasted_iota(jnp.int32, (512, 256), 1)
        kept = jnp.where(own_slot[...] == (lane & 127) >> 4, shrunk[...], 0.0).astype(BF)
        fold = one_hot((256, 128), lambda r, c: (r & 15 | (r >> 7) << 4) == c)
        kept = jnp.dot(kept, fold, preferred_element_type=F32)
        kept = kept.T.astype(BF)[:32]
        picked[...] = jnp.dot(kept, get[...], preferred_element_type=F32).astype(BF)


def in_hbm(v):
    return pltpu.with_memory_space_constraint(v, pltpu.HBM)


def one_hot(shape, test):
    r = lax.broadcasted_iota(jnp.int32, shape, 0)
    c = lax.broadcasted_iota(jnp.int32, shape, 1)
    return jnp.where(test(r, c), 1.0, 0.0).astype(BF)


def hidden_kernel(gate, up, shrunk, get, row_request, gate_rows, up_rows, down_cols, out):
    last = (((1,), (1,)), ((), ()))
    low = lax.dot_general(get[...], shrunk[...], last, preferred_element_type=F32).astype(BF)
    wide = one_hot((2 * R, 256), lambda r, c: (c & 15 | (c >> 7) << 4) == r)
    low = jnp.dot(low, wide, preferred_element_type=F32)
    lane = lax.broadcasted_iota(jnp.int32, (512, 256), 1)
    hot = row_request[...] == (lane & 127) >> 4
    low = jnp.where(hot, low, 0.0).astype(BF)
    g = gate[...] + lax.dot_general(low[:, :128], gate_rows[...], last, preferred_element_type=F32)
    u = up[...] + lax.dot_general(low[:, 128:], up_rows[...], last, preferred_element_type=F32)
    hidden = (g / (1.0 + jnp.exp(-g)) * u).astype(BF)
    down = jnp.dot(hidden, down_cols[...], preferred_element_type=F32)
    down = jnp.where(hot[:, :128], down, 0.0).astype(BF)
    units = hidden.shape[1]
    place = one_hot((units, 256), lambda r, c: r == c)
    after = one_hot((128, 256), lambda r, c: (r & 15) + units == c)
    both = jnp.dot(hidden, place, preferred_element_type=F32)
    both = (both + jnp.dot(down, after, preferred_element_type=F32)).astype(BF)
    first = (((0,), (0,)), ((), ()))
    out[...] = lax.dot_general(get[...], both, first, preferred_element_type=F32).astype(BF)


def hidden_of(*args):
    return pl.pallas_call(
        hidden_kernel,
        out_shape=jax.ShapeDtypeStruct((512, 256), BF),
        compiler_params=pltpu.CompilerParams(vmem_limit_bytes=12 << 20),
        name="hidden",
    )(*args)


def products(p, q, w_gate, w_up, a_gate, a_up, own_slot, get):
    half = p[0].shape[1]
    steps = half // KB
    rows = [pl.BlockSpec((v.shape[0], KB), lambda k: (0, jnp.minimum(k, steps - 1))) for v in p]
    rows += [pl.BlockSpec((v.shape[0], KB), lambda k: (0, jnp.maximum(k - steps, 0))) for v in q]
    units = w_gate.shape[1]
    cols = [pl.BlockSpec((units, KB), lambda k: (0, k))] * 2
    cols += [pl.BlockSpec((KB, 128), lambda k: (k, 0))] * 2
    cols += [pl.BlockSpec((512, 1), lambda k: (0, 0)), pl.BlockSpec((512, 512), lambda k: (0, 0))]
    return pl.pallas_call(
        products_kernel,
        grid=(2 * steps,),
        in_specs=rows + cols,
        out_specs=[
            pl.BlockSpec((512, units), lambda k: (0, 0)),
            pl.BlockSpec((512, units), lambda k: (0, 0)),
            pl.BlockSpec((2 * R, 512), lambda k: (0, 0)),
        ],
        out_shape=[
            pltpu.HBM((512, units), F32),
            pltpu.HBM((512, units), F32),
            jax.ShapeDtypeStruct((2 * R, 512), BF),
        ],
        scratch_shapes=[pltpu.VMEM((512, 256), F32)],
        compiler_params=pltpu.CompilerParams(vmem_limit_bytes=36 << 20),
        name="products",
    )(*p, *q, in_hbm(w_gate.T), in_hbm(w_up.T), in_hbm(a_gate), in_hbm(a_up), own_slot, get)


def row_order(me, order):
    row = jnp.arange(512, dtype=jnp.int32)
    at = {}
    at[order[0]] = (me[order[0]] - (row >> 2)) & 3
    at[order[1]] = (me[order[1]] - (row >> 4)) & 3
    at[order[2]] = (me[order[2]] - (row >> 6)) & 3
    at["c"] = (me["c"] + (row >> 8)) & 1
    return (at["y"] << 7) | (at["c"] << 6) | (at["x"] << 4) | (at["z"] << 2) | (row & 3)


def block(v, at):
    return lax.dynamic_index_in_dim(v, at, 0, keepdims=False)


def local(
    tokens_in,
    w_gate,
    w_up,
    w_down,
    a_gate,
    a_up,
    b_gate,
    b_up,
    a_down,
    b_down,
    lengths,
    request_adapter,
    placement,
):
    me = coords()
    D = tokens_in.shape[1]

    half = D // 2
    v = jnp.concatenate(gather4(tokens_in, "z"), axis=0)
    p = jnp.concatenate(gather4(v[:, :half], "x"), axis=0)
    q = jnp.concatenate(gather4(v[:, half:], "y"), axis=0)
    p, q, lengths, request_adapter, placement, ten, adp = lax.optimization_barrier(
        (p, q, lengths, request_adapter, placement, lax.axis_index("tensor"), lax.axis_index("adapter"))
    )
    me = {"y": ten >> 1, "c": ten & 1, "x": adp >> 2, "z": adp & 3}
    p, q = gather4(p, "y"), gather4(q, "x")
    p = p + [shift(v, "c", 1) for v in p]
    q = q + [shift(v, "c", 1) for v in q]

    positions = jnp.arange(512, dtype=jnp.int32)
    ends = jnp.sum(
        jnp.where(jnp.arange(8)[:, None] <= jnp.arange(8)[None, :], lengths[:, None], 0), axis=0
    )
    request = jnp.sum((positions[:, None] >= ends[None, :]).astype(jnp.int32), axis=1)
    adapter_hot = request_adapter[:, None] == jnp.arange(128, dtype=jnp.int32)[None, :]
    slots = jnp.sum(jnp.where(adapter_hot, placement[None, :], 0), axis=1)

    slot_r = jnp.sum(jnp.where(jnp.arange(8) == ten, slots, 0))
    rows_b = lax.dynamic_slice_in_dim(b_down, (slot_r & 7) * R, R, axis=0)
    rows_b = jnp.where(slot_r >> 3 == adp, rows_b, jnp.zeros_like(rows_b))
    rows_b = rows_b.reshape(R, 4, 4, 512).transpose(2, 1, 0, 3)
    got = [block(rows_b, me["z"])]
    got += [shift(block(rows_b, (me["z"] + s) & 3), "z", s) for s in (1, 2, 3)]
    rows_b = sum(v.astype(F32) for v in got).astype(BF)
    blk = jnp.arange(8, dtype=jnp.int32)
    blk_request = ((me["y"] - blk) & 3) << 1 | (me["c"] + (blk >> 2)) & 1

    unit = jnp.concatenate(
        [jnp.zeros((224, 128), BF), jnp.eye(R, 128, dtype=BF), jnp.zeros((16, 128), BF)], axis=0
    )
    w_blocks = w_down.reshape(16, 224, 512)

    tok = jnp.arange(512, dtype=jnp.int32)
    held = row_order(me, ("z", "x", "y"))
    get = (held[:, None] == tok[None, :]).astype(BF)
    row_request = jnp.sum((held[:, None] >= ends[None, :]).astype(jnp.int32), axis=1)
    row_slot = jnp.sum(
        jnp.where(row_request[:, None] == jnp.arange(8)[None, :], slots[None, :], 0), axis=1
    )
    own_slot = jnp.where(row_slot >> 3 == adp, row_slot & 7, -1)

    gate, up, picked = products(
        p, q, w_gate, w_up, a_gate, a_up, own_slot[:, None], get
    )

    picked, request_adapter = lax.optimization_barrier((picked, request_adapter))
    wide = jnp.arange(2048, dtype=jnp.int32)
    rank = jnp.arange(128, dtype=jnp.int32)
    own_adapter = jnp.sum(
        jnp.where((rank >> 4)[:, None] == jnp.arange(8)[None, :], request_adapter[None, :], 0), axis=1
    )
    pick = (wide[:, None] == ((own_adapter << 4) | (rank & 15))[None, :]).astype(BF)
    take = (((0,), (0,)), ((), ()))
    gate_rows = lax.dot_general(b_gate, pick, take, preferred_element_type=F32).astype(BF)
    up_rows = lax.dot_general(b_up, pick, take, preferred_element_type=F32).astype(BF)
    down_cols = jnp.dot(a_down, pick, preferred_element_type=F32).astype(BF)

    picked = sum(v.astype(F32) for v in gather4(picked, "z")).astype(BF)
    sent = [
        jnp.concatenate([picked, block(rows_b, (me["x"] + s) & 3)], axis=0) for s in range(4)
    ]
    got = [sent[0]] + [shift(sent[s], "x", s) for s in (1, 2, 3)]
    both = sum(v.astype(F32) for v in got).astype(BF)
    picked, rows_b = both[: 2 * R], both[2 * R :]
    hidden = hidden_of(in_hbm(gate), in_hbm(up), picked, get, row_request[:, None], gate_rows, up_rows, down_cols)

    def spread_block(low, hot):
        return jnp.where(hot[:, :, None], low[:, None, :], jnp.zeros_like(low)[:, None, :]).reshape(
            low.shape[0], -1
        )

    ways = (("x", "z"), ("z", "x"))
    first = [gather4(hidden[i * 256 : i * 256 + 256], way[0]) for i, way in enumerate(ways)]
    first[0][1], rows_b = lax.optimization_barrier((first[0][1], rows_b))
    rows_b = jnp.concatenate(gather4(rows_b, "y"), axis=0)
    first = lax.optimization_barrier([jnp.stack(v, axis=0) for v in first])
    pieces = [ring4(h, way[1]) for h, way in zip(first, ways)]
    rows_b = jnp.concatenate([rows_b, shift(rows_b, "c", 1)], axis=0)
    base = []
    for (own, near, low_half, high_half, far), way in zip(pieces, ways):
        acc = 0.0
        for r2, piece in ((0, own), (1, near), (3, far), (2, low_half), (2, high_half)):
            for i in range(piece.shape[0]):
                r1 = i + 2 if piece is high_half else i
                at = {way[0]: (me[way[0]] - r1) & 3, way[1]: (me[way[1]] - r2) & 3}
                w = block(w_blocks, at["x"] << 2 | at["z"])
                w = jnp.concatenate([w, jnp.zeros((32, 512), BF)], axis=0)
                w = jnp.concatenate([w, unit], axis=1)
                acc = acc + jnp.dot(piece[i], w, preferred_element_type=F32)
        base.append(acc)
    base = jnp.concatenate(base, axis=0)
    hot_blk = request[:, None] == blk_request[None, :]
    delta = jnp.dot(
        spread_block(base[:, 512 : 512 + R].astype(BF), hot_blk), rows_b, preferred_element_type=F32
    )
    out = (base[:, :512] + delta).reshape(4, 2, 64, 512)

    got = shift(jnp.where(me["c"] == 0, out[:, 1], out[:, 0]).astype(BF), "c", 1)
    out = jnp.where(me["c"] == 0, out[:, 0], out[:, 1]) + got.astype(F32)
    out = out.astype(BF).reshape(64, 4, 512)
    same = [[(2 * y + c) * 16 + a for y in range(4) for a in range(16)] for c in range(2)]
    got = lax.all_to_all(
        out, ("tensor", "adapter"), 0, 0, tiled=True, axis_index_groups=same
    )
    mixed = jnp.sum(got.reshape(4, 16, 4, 512).astype(F32), axis=0).astype(BF)
    return mixed.transpose(1, 0, 2).reshape(4, D)


def solution(mesh):
    in_specs = (
        P(("tensor", "adapter"), None),
        P(None, ("tensor", "adapter")),
        P(None, ("tensor", "adapter")),
        P("tensor", "adapter"),
        P(None, "adapter"),
        P(None, "adapter"),
        P(None, ("tensor", "adapter")),
        P(None, ("tensor", "adapter")),
        P(("tensor", "adapter"), None),
        P("adapter", None),
        P(),
        P(),
        P(),
    )
    out_specs = P(("tensor", "adapter"), None)
    return jax.shard_map(local, mesh=mesh, in_specs=in_specs, out_specs=out_specs, check_vma=False)
```
